256 devices in a mesh: gx: 8 (over x, core), gy: 16 (over y_lo, z), gz: 2 (over y_hi).
Axes of the slice: x: 4, y: 4 (y_hi: 2, y_lo: 2; y = y_hi * 2 + y_lo), z: 8, core: 2. Of those that a mesh axis runs over, the one named last changes fastest.
Arguments:
- probes: float32 [8, 64, 256, 512], P(None, 'gx', 'gy', 'gz'), may hold values from -0.011 to 0.011
- kappa2: float32 [64, 256, 512], P('gx', 'gy', 'gz'), may hold values from 0.25 to 4
- cotangents: float32 [5, 8], replicated, may hold values from -0.4375 to 0.4375
Outputs:
- kappa_grad: float32 [64, 256, 512], P('gx', 'gy', 'gz')
The draws below stay inside these ranges and needn't reach their ends.
All inputs are finite; a program needn't handle non-finite values.
Results may differ from the reference program's by a relative error of at most 0.02.
Values sent between devices are 32-bit elements; how exact they have to be, the bound alone decides.
A program may use at most 64 MiB of HBM per device.

```python
import math
import jax
import jax.numpy as jnp
from jax import lax

P_SIZE = 8
NX = 64
NY = 256
NZ = 512


PROBE_SCALE = 0.00035


def draw_probes(key, part):
    first = jnp.arange(NX, dtype=jnp.float32) / max(NX - 1, 1)
    second = jnp.arange(NY, dtype=jnp.float32) / max(NY - 1, 1)
    third = jnp.arange(NZ, dtype=jnp.float32) / max(NZ - 1, 1)
    envelope = jnp.sqrt((1.0 + 2.0 * first)[:, None, None] * (1.0 + 2.0 * second)[None, :, None] * (1.0 + 2.0 * third)[None, None, :])
    values = jax.random.truncated_normal(key, -6.0, 6.0, (P_SIZE, NX, NY, NZ), jnp.float32)
    return (values * envelope[None] * PROBE_SCALE).astype(jnp.float32)


def steps_of(key, shape, pieces, smallest, top_value):
    level = 1.0
    for axis_at, blocks in pieces:
        steps = jax.random.uniform(jax.random.fold_in(jax.random.fold_in(key, 6), axis_at), (blocks,), jnp.float32, smallest / len(pieces), top_value / len(pieces))
        level = level * jnp.repeat(jnp.exp(steps), shape[axis_at] // blocks).reshape((-1,) + (1,) * (len(shape) - 1 - axis_at))
    return level


def scatter_about(rng, shape, width, most, kind=jnp.bfloat16):
    return jnp.clip(width * jax.random.normal(rng, shape, jnp.float32), -most, most).astype(kind)


def setup_inputs(seed: int = 0) -> dict:
    key_list = jax.random.split(jax.random.key(seed), 4)
    probes = draw_probes(jax.random.fold_in(key_list[3], 71), 0)
    kappa2 = jnp.clip(jnp.exp(math.log(4.0) - 2.7725887 * jax.random.uniform(key_list[1], (NX, NY, NZ), jnp.float32) ** steps_of(key_list[1], (NX, NY, NZ), ((0, 8), (1, 16), (2, 2)), -0.2, 0.2)), 0.25, 4.0)
    cotangents = scatter_about(key_list[2], (5, P_SIZE), 0.03, 0.4375, jnp.float32)
    return dict(probes=probes, kappa2=kappa2, cotangents=cotangents)


EPSILON = 1e-06

def stencil_apply(field, kappa2):
    padded = jnp.pad(field, 1)
    total = padded[2:, 1:-1, 1:-1] + padded[:-2, 1:-1, 1:-1]
    total = total + padded[1:-1, 2:, 1:-1] + padded[1:-1, :-2, 1:-1]
    total = total + padded[1:-1, 1:-1, 2:] + padded[1:-1, 1:-1, :-2]
    return (6.0 + kappa2) * field - total

def squared_apply(field, kappa2):
    return stencil_apply(stencil_apply(field, kappa2), kappa2)

def lanczos_loss(kappa2, probe, weights):
    first_basis = probe / jnp.sqrt(jnp.mean(probe * probe) + EPSILON)
    first_image = squared_apply(first_basis, kappa2)
    first_alpha = jnp.mean(first_basis * first_image)
    first_rest = first_image - first_alpha * first_basis
    first_beta = jnp.sqrt(jnp.mean(first_rest * first_rest) + EPSILON)
    second_basis = first_rest / first_beta
    second_image = squared_apply(second_basis, kappa2) - first_beta * first_basis
    second_alpha = jnp.mean(second_basis * second_image)
    second_rest = second_image - second_alpha * second_basis
    second_beta = jnp.sqrt(jnp.mean(second_rest * second_rest) + EPSILON)
    third_basis = second_rest / second_beta
    third_image = squared_apply(third_basis, kappa2) - second_beta * second_basis
    third_alpha = jnp.mean(third_basis * third_image)
    return weights[0] * first_alpha + weights[1] * second_alpha + weights[2] * third_alpha + weights[3] * first_beta + weights[4] * second_beta

def reference(probes, kappa2, cotangents):
    gradient_fn = jax.grad(lanczos_loss)

    def accumulate(index, total):
        return total + gradient_fn(kappa2, probes[index], cotangents[:, index])
    total = lax.fori_loop(0, P_SIZE, accumulate, jnp.zeros_like(kappa2))
    return total * float(NX * NY * NZ)
```

```python
import functools

import jax
import jax.numpy as jnp
from jax import lax
from jax.experimental import pallas as pl
from jax.experimental.pallas import tpu as pltpu
from jax.sharding import PartitionSpec as P

EPSILON = 1e-06
MESH = pl.DeviceIdType.MESH
NP, NX, NY, NZ = 8, 8, 16, 256
ZL, ZH = 16, 16
ROWS = NY * ZL
TOP = 8
LAST = 9
ZERO = (LAST + 1) * NX


def scalars(gram, shifts, cot):
    pp, pap, vv, vav, ww, waw = gram
    sig, tau, rho = shifts
    s0 = pp + EPSILON
    a1 = pap / s0
    pv = pap - sig * pp
    d = sig - a1
    b1s = (vv + 2.0 * d * pv + d * d * pp) / s0 + EPSILON
    b1 = jnp.sqrt(b1s)
    scale = s0 * b1s
    pav = vv + sig * pv
    a2 = (vav + 2.0 * d * pav + d * d * pap) / scale - (pv + d * pp) / s0
    b = tau + d - a2
    a = rho + d * sig - b1s - a2 * d
    pw = vv + (sig - tau) * pv - rho * pp
    vw = vav - tau * vv - rho * pv
    b2s = (ww + b * b * vv + a * a * pp + 2.0 * (b * vw + a * pw + a * b * pv)) / scale + EPSILON
    b2 = jnp.sqrt(b2s)
    vaw = ww + tau * vw + rho * pw
    paw = vw + sig * pw
    top = waw + b * b * vav + a * a * pap + 2.0 * (b * vaw + a * paw + a * b * pav)
    cross = vw + b * vv + a * pv + d * (pw + b * pv + a * pp)
    a3 = top / (scale * b2s) - cross / scale
    return cot[0] * a1 + cot[1] * a2 + cot[2] * a3 + cot[3] * b1 + cot[4] * b2


def swap_rows_lanes(arrays, lane):
    arrays = list(arrays)
    for s in (1, 2, 4, 8):
        low = (lane & s) == 0
        for i in range(16):
            if i & s:
                continue
            one, two = arrays[i], arrays[i + s]
            arrays[i] = jnp.where(low, one, pltpu.roll(two, s, 1))
            arrays[i + s] = jnp.where(low, pltpu.roll(one, 128 - s, 1), two)
    return arrays


def kernel(
    sizes, probes_ref, kappa_ref, cot_ref, out_ref,
    u, k2, g, pv, kv, ov, hx, hy, hz, zs, zm, zp, ars, arr,
    lsem, ssem, rsem, asem, bsem,
):
    nx, ny, nz = sizes
    gx, gy, gz = lax.axis_index("gx"), lax.axis_index("gy"), lax.axis_index("gz")
    inverse_count = 1.0 / (nx * NX * ny * NY * nz * NZ)

    load_p = pltpu.make_async_copy(probes_ref, pv, lsem.at[0])
    load_k = pltpu.make_async_copy(kappa_ref, kv, lsem.at[1])
    load_p.start()
    load_k.start()

    barrier = pltpu.get_barrier_semaphore()
    group_one = [(i, j) for i in range(nx) for j in range(nz)]
    for i, j in group_one:
        @pl.when(jnp.logical_or(gx != i, gz != j))
        def _():
            pl.semaphore_signal(barrier, inc=1, device_id={"gx": i, "gz": j}, device_id_type=MESH)
    for j in range(ny):
        @pl.when(gy != j)
        def _():
            pl.semaphore_signal(barrier, inc=1, device_id={"gy": j}, device_id_type=MESH)

    lane = lax.broadcasted_iota(jnp.int32, (16, 128), 1)
    zh = lane & 15
    lane8 = lax.broadcasted_iota(jnp.int32, (8, 128), 1)
    sub8 = lax.broadcasted_iota(jnp.int32, (8, 128), 0)
    lane1 = lax.broadcasted_iota(jnp.int32, (1, 128), 1)
    zero_tile = jnp.zeros((8, 128), jnp.float32)

    def clear(i, _):
        u[ZERO, pl.ds(TOP + i * 16, 16), :] = jnp.zeros((16, 128), jnp.float32)
        return 0
    lax.fori_loop(0, 16, clear, 0)

    def clear_pads(i, _):
        u[i, 0:8, :] = zero_tile
        u[i, TOP + ROWS : TOP + ROWS + 8, :] = zero_tile
        return 0
    lax.fori_loop(0, LAST * NX, clear_pads, 0)
    def clear_z(i, _):
        zm[i, 16:24, :] = zero_tile
        zp[i, 0:8, :] = zero_tile
        return 0
    lax.fori_loop(0, NX, clear_z, 0)

    load_p.wait()

    def turn_probes(x, _):
        block = pv[:, x].reshape(NP * NY, NZ)
        halves = [block[:, :128].T, block[:, 128:].T]
        rows = [halves[i // 8][(i % 8) * 16 : (i % 8) * 16 + 16, :] for i in range(16)]
        rows = swap_rows_lanes(rows, lane)
        for y in range(NY):
            u[x, TOP + y * ZL : TOP + y * ZL + ZL, :] = rows[y]
        return 0
    lax.fori_loop(0, NX, turn_probes, 0)

    def copies(f):
        lo, hi = f * NX, f * NX + NX - 1
        both = pl.ds(lo, NX)
        return (
            (gx > 0, pltpu.make_async_remote_copy(
                u.at[lo, pl.ds(TOP, ROWS)], hx.at[f, 1], ssem.at[f, 0], rsem.at[f, 1],
                device_id={"gx": gx - 1}, device_id_type=MESH)),
            (gx < nx - 1, pltpu.make_async_remote_copy(
                u.at[hi, pl.ds(TOP, ROWS)], hx.at[f, 0], ssem.at[f, 1], rsem.at[f, 0],
                device_id={"gx": gx + 1}, device_id_type=MESH)),
            (gy > 0, pltpu.make_async_remote_copy(
                u.at[both, pl.ds(TOP, ZL)], hy.at[f, 1], ssem.at[f, 2], rsem.at[f, 3],
                device_id={"gy": gy - 1}, device_id_type=MESH)),
            (gy < ny - 1, pltpu.make_async_remote_copy(
                u.at[both, pl.ds(TOP + ROWS - ZL, ZL)], hy.at[f, 0], ssem.at[f, 3], rsem.at[f, 2],
                device_id={"gy": gy + 1}, device_id_type=MESH)),
            (None, pltpu.make_async_remote_copy(
                zs.at[f], hz.at[f], ssem.at[f, 4], rsem.at[f, 4],
                device_id={"gz": 1 - gz}, device_id_type=MESH)),
        )

    edge = (ZL - 1) * (1 - gz)
    edge8 = (ZH - 1) * (1 - gz)

    def z_faces(f):
        if f > 0:
            copies(f - 1)[4][1].wait_recv()
            came = hz[f - 1]
            came = jnp.where(gz == 0, pltpu.roll(came, 15, 1), pltpu.roll(came, 128 - 15, 1))
        pack = zero_tile
        for x in range(NX):
            for t in range(2):
                k = 2 * x + t
                at = (f * NX + x, pl.ds(TOP + edge + t * 8 * ZL, 8, ZL), slice(None))
                row = u[at]
                if f > 0:
                    row = row - jnp.where(
                        (lane8 & 15) == edge8, pltpu.roll(came, (128 - k) % 128, 1), 0.0)
                    u[at] = row
                if f < LAST:
                    moved = pltpu.roll(row, k, 1) if k else row
                    pack = jnp.where(((lane8 - edge8 - k) & 15) == 0, moved, pack)
        if f < LAST:
            zs[f] = pack

    def z_carry(f):
        def one(x, _):
            top = u[f * NX + x, pl.ds(TOP + ZL - 1, NY, ZL), :]
            low = u[f * NX + x, pl.ds(TOP, NY, ZL), :]
            zm[x, 0:16, :] = jnp.where(zh == 0, 0.0, pltpu.roll(top, 1, 1))
            zp[x, 8:24, :] = jnp.where(zh == ZH - 1, 0.0, pltpu.roll(low, 127, 1))
            return 0
        lax.fori_loop(0, NX, one, 0)

    first = sub8 == 0
    final = sub8 == 7

    def main(f, moment, last):
        def one(x, acc):
            s = f * NX + x
            below = jnp.where(x == 0, ZERO, s - 1)
            above = jnp.where(x == NX - 1, ZERO, s + 1)
            tiles = {}
            for y in range(NY):
                for t in range(2):
                    for yy in (y, y + 1):
                        if yy < NY and (yy, t) not in tiles:
                            tiles[yy, t] = u[s, TOP + yy * ZL + t * 8 : TOP + yy * ZL + t * 8 + 8, :]
                for t in range(2):
                    r = y * ZL + t * 8
                    here = tiles[y, t]
                    total = u[below, TOP + r : TOP + r + 8, :] + u[above, TOP + r : TOP + r + 8, :]
                    if y > 0:
                        total = total + tiles[y - 1, t]
                    if y < NY - 1:
                        total = total + tiles[y + 1, t]
                    under = u[s, TOP + r - 1 : TOP + r + 7, :]
                    over = u[s, TOP + r + 1 : TOP + r + 9, :]
                    if t == 0:
                        under = jnp.where(first, zm[x, y : y + 8, :], under)
                    else:
                        over = jnp.where(final, zp[x, y + 1 : y + 9, :], over)
                    total = total + (under + over)
                    value = k2[x, r : r + 8, :] * here - total
                    u[s + NX, TOP + r : TOP + r + 8, :] = value
                    if moment:
                        acc = acc + here * here
            return acc
        return lax.fori_loop(0, NX, one, zero_tile)

    def faces(f):
        todo = copies(f)
        for ok, slot, slab in ((gx > 0, 0, 0), (gx < nx - 1, 1, NX - 1)):
            @pl.when(ok)
            def _():
                todo[1 - slot][1].wait_recv()
                at = (f + 1) * NX + slab
                u[at, TOP : TOP + ROWS, :] = u[at, TOP : TOP + ROWS, :] - hx[f, slot]
        for ok, slot, r in ((gy > 0, 0, TOP), (gy < ny - 1, 1, TOP + ROWS - ZL)):
            @pl.when(ok)
            def _():
                todo[3 - slot][1].wait_recv()
                at = (pl.ds((f + 1) * NX, NX), slice(r, r + ZL), slice(None))
                u[at] = u[at] - hy[f, slot]

    def start(f, which):
        todo = copies(f)
        for i in which:
            ok, copy = todo[i]
            if ok is None:
                copy.start()
            else:
                @pl.when(ok)
                def _():
                    copy.start()

    me_one, me_two = gx * nz + gz, gy

    def phase_copies(n):
        out = []
        if n % 2 == 0:
            for i, j in group_one:
                out.append((jnp.logical_or(gx != i, gz != j), i * nz + j, {"gx": i, "gz": j}))
            me = me_one
        else:
            for j in range(ny):
                out.append((gy != j, j, {"gy": j}))
            me = me_two
        return [
            (ok, slot, pltpu.make_async_remote_copy(
                ars.at[n], arr.at[n, me], asem.at[n, slot], bsem.at[n, me],
                device_id=where, device_id_type=MESH),
             pltpu.make_async_remote_copy(
                ars.at[n], arr.at[n, slot], asem.at[n, slot], bsem.at[n, slot],
                device_id=where, device_id_type=MESH))
            for ok, slot, where in out
        ]

    def phase_start(n, value):
        ars[n] = value
        for ok, _, copy, _ in phase_copies(n):
            @pl.when(ok)
            def _():
                copy.start()

    def phase_end(n):
        me = me_one if n % 2 == 0 else me_two
        arr[n, me] = ars[n]
        for ok, _, _, copy in phase_copies(n):
            @pl.when(ok)
            def _():
                copy.wait_recv()
        parts = [arr[n, i] for i in range(16)]
        while len(parts) > 1:
            parts = [parts[i] + parts[i + 1] for i in range(0, len(parts), 2)]
        return parts[0]

    def stack(rows):
        tile = zero_tile
        for i, row in enumerate(rows):
            tile = jnp.where(sub8 == i, jnp.sum(row, axis=0, keepdims=True), tile)
        return tile

    def over_lanes(tile):
        for s in (1, 2, 4, 8):
            low = (lane8 & s) == 0
            tile = tile + jnp.where(low, pltpu.roll(tile, 128 - s, 1), pltpu.roll(tile, s, 1))
        return tile * inverse_count

    pl.semaphore_wait(barrier, nx * nz - 1 + ny - 1)
    start(0, (0, 1, 2, 3))
    z_faces(0)
    start(0, (4,))

    load_k.wait()
    block = kv[...].reshape(NX * NY, NZ)
    halves = [block[:, :128].T, block[:, 128:].T]
    rows = [halves[i // 8][(i % 8) * 16 : (i % 8) * 16 + 16, :] for i in range(16)]
    rows = swap_rows_lanes(rows, lane)
    for y in range(NY):
        g[0, y * ZL : y * ZL + ZL, :] = rows[y] + 6.0

    def spread(y, _):
        row = g[0, pl.ds(y * ZL, ZL), :]
        for x in range(NX):
            one = row if x == 0 else pltpu.roll(row, 128 - 16 * x, 1)
            one = jnp.where(lane < 16, one, 0.0)
            for s in (16, 32, 64):
                one = one + pltpu.roll(one, s, 1)
            k2[x, pl.ds(y * ZL, ZL), :] = one
        return 0
    lax.fori_loop(0, NY, spread, 0)

    def step(f, moment=False):
        z_carry(f)
        return main(f, moment, False)

    def finish(f):
        faces(f)
        z_faces(f + 1)
        if f + 1 < LAST:
            start(f + 1, (0, 1, 2, 3, 4))

    moments = []
    for f in range(4):
        moments.append(step(f, True))
        if f < 3:
            finish(f)
    phase_start(0, stack(moments))
    finish(3)

    step(4)
    phase_start(1, phase_end(0))
    finish(4)

    step(5)
    raw = over_lanes(phase_end(1))
    m = [raw[i : i + 1, :] for i in range(4)]
    s0 = m[0] + EPSILON
    sig = m[1] / s0
    vv = jnp.maximum(m[2] - 2.0 * sig * m[1] + sig * sig * m[0], 0.0)
    rho = jnp.clip(vv / s0 + EPSILON, 0.0, 65536.0)
    tau = (m[3] - 2.0 * sig * m[2] + sig * sig * m[1]) / (s0 * rho) - (m[1] - sig * m[0]) / s0
    tau = jnp.clip(tau, 0.0, 256.0)
    e1 = -(sig + tau)
    e0 = sig * tau - rho

    def refine(x, acc):
        av, akv, aw, akw = acc
        for r in range(0, ROWS, 8):
            at = slice(TOP + r, TOP + r + 8)
            t = [u[i * NX + x, at, :] for i in range(6)]
            v = t[2] - sig * t[0]
            kv_ = t[3] - sig * t[1]
            w = (t[4] + e1 * t[2]) + e0 * t[0]
            kw = (t[5] + e1 * t[3]) + e0 * t[1]
            av, akv, aw, akw = av + v * v, akv + kv_ * kv_, aw + w * w, akw + kw * kw
        return av, akv, aw, akw
    phase_start(2, stack(lax.fori_loop(0, NX, refine, (zero_tile,) * 4)))
    finish(5)

    step(6)
    phase_start(3, phase_end(2))
    finish(6)

    step(7)
    fine = over_lanes(phase_end(3))
    cot = []
    for i in range(5):
        row = jnp.zeros((1, 128), jnp.float32)
        for p in range(NP):
            row = jnp.where((lane1 >> 4) == p, cot_ref[i, p], row)
        cot.append(row)
    gram = (m[0], m[1], fine[0:1], fine[1:2], fine[2:3], fine[3:4])
    _, back = jax.vjp(lambda *q: scalars(q, (sig, tau, rho), cot), *gram)
    _, gpap, gvv, gvav, gww, gwaw = back(jnp.ones((1, 128), jnp.float32))
    sq = e1 * e1 + 2.0 * e0
    c5 = 2.0 * gwaw
    c4 = 2.0 * (gww + 2.0 * e1 * gwaw)
    c3 = 2.0 * (gvav + 2.0 * e1 * gww + sq * gwaw)
    c2 = 2.0 * (gvv - 2.0 * sig * gvav + sq * gww + 2.0 * e1 * e0 * gwaw)
    c1 = 2.0 * (gpap - 2.0 * sig * gvv + sig * sig * gvav + 2.0 * e1 * e0 * gww + e0 * e0 * gwaw)
    finish(7)

    def part(x, _):
        for r in range(0, ROWS, 8):
            at = slice(TOP + r, TOP + r + 8)
            t = [u[i * NX + x, at, :] for i in range(9)]
            value = c1 * (t[0] * t[1])
            value = value + c2 * (t[0] * t[3] + t[1] * t[2])
            value = value + c3 * (t[0] * t[5] + t[1] * t[4] + t[2] * t[3])
            value = value + c4 * ((t[0] * t[7] + t[1] * t[6]) + (t[2] * t[5] + t[3] * t[4]))
            value = value + c5 * ((t[1] * t[8] + t[2] * t[7]) + (t[3] * t[6] + t[4] * t[5]))
            g[x, r : r + 8, :] = value
        return 0

    step(8)
    lax.fori_loop(0, NX, part, 0)
    finish(8)

    def gather(y, _):
        r = pl.ds(y * ZL, ZL)
        ru = pl.ds(TOP + y * ZL, ZL)
        t = [g[x, r, :] + c5 * (u[x, ru, :] * u[LAST * NX + x, ru, :]) for x in range(NX)]
        low = (lane & 64) == 0
        t = [jnp.where(low, t[i], t[i + 4]) + pltpu.roll(jnp.where(low, t[i + 4], t[i]), 64, 1)
             for i in range(4)]
        for s, n in ((32, 2), (16, 1)):
            low = (lane & s) == 0
            t = [jnp.where(low, t[i] + pltpu.roll(t[i], 128 - s, 1), t[i + n] + pltpu.roll(t[i + n], s, 1))
                 for i in range(n)]
        g[0, r, :] = t[0]
        return 0
    lax.fori_loop(0, NY, gather, 0)
    rows = [g[0, y * ZL : y * ZL + ZL, :] for y in range(NY)]
    rows = swap_rows_lanes(rows, lane)
    for h in range(2):
        half = jnp.concatenate(rows[h * 8 : h * 8 + 8], axis=0).T
        ov[:, :, h * 128 : h * 128 + 128] = half.reshape(NX, NY, 128)
    store = pltpu.make_async_copy(ov, out_ref, lsem.at[2])
    store.start()

    for f in range(LAST):
        for ok, copy in copies(f):
            if ok is None:
                copy.wait_send()
            else:
                @pl.when(ok)
                def _():
                    copy.wait_send()
    for n in range(4):
        for ok, _, copy, _ in phase_copies(n):
            @pl.when(ok)
            def _():
                copy.wait_send()
    store.wait()


def body(probes, kappa2, cotangents):
    sizes = tuple(lax.axis_size(a) for a in ("gx", "gy", "gz"))
    f32 = jnp.float32
    any_space = pl.BlockSpec(memory_space=pl.ANY)
    return pl.pallas_call(
        functools.partial(kernel, sizes),
        out_shape=jax.ShapeDtypeStruct((NX, NY, NZ), f32),
        in_specs=[any_space, any_space, pl.BlockSpec(memory_space=pltpu.SMEM)],
        out_specs=any_space,
        scratch_shapes=[
            pltpu.VMEM((ZERO + 1, TOP + ROWS + 8, 128), f32),
            pltpu.VMEM((NX, ROWS, 128), f32),
            pltpu.VMEM((NX, ROWS, 128), f32),
            pltpu.VMEM((NP, NX, NY, NZ), f32),
            pltpu.VMEM((NX, NY, NZ), f32),
            pltpu.VMEM((NX, NY, NZ), f32),
            pltpu.VMEM((LAST, 2, ROWS, 128), f32),
            pltpu.VMEM((LAST, 2, NX, ZL, 128), f32),
            pltpu.VMEM((LAST, 8, 128), f32),
            pltpu.VMEM((LAST, 8, 128), f32),
            pltpu.VMEM((NX, 24, 128), f32),
            pltpu.VMEM((NX, 24, 128), f32),
            pltpu.VMEM((4, 8, 128), f32),
            pltpu.VMEM((4, 16, 8, 128), f32),
            pltpu.SemaphoreType.DMA((3,)),
            pltpu.SemaphoreType.DMA((LAST, 5)),
            pltpu.SemaphoreType.DMA((LAST, 5)),
            pltpu.SemaphoreType.DMA((4, 16)),
            pltpu.SemaphoreType.DMA((4, 16)),
        ],
        compiler_params=pltpu.CompilerParams(
            collective_id=0, has_side_effects=True, vmem_limit_bytes=40 << 20
        ),
    )(probes, kappa2, cotangents)


def solution(mesh):
    return jax.shard_map(
        body,
        mesh=mesh,
        in_specs=(P(None, "gx", "gy", "gz"), P("gx", "gy", "gz"), P()),
        out_specs=P("gx", "gy", "gz"),
        check_vma=False,
    )
```

```python
import functools

import jax
import jax.numpy as jnp
from jax import lax
from jax.experimental import pallas as pl
from jax.experimental.pallas import tpu as pltpu
from jax.sharding import PartitionSpec as P

EPSILON = 1e-06
MESH = pl.DeviceIdType.MESH
NP, NX, NY, NZ = 8, 8, 16, 256
GROUPS, GP = 2, 4
ZL, ZH = 8, 32
TOP = 8
EDGE = 2
SLABS, TILES = NX + 2 * EDGE, 24
ROWS = TOP + TILES * ZL + 8
LAST = 9


def scalars(gram, shifts, cot):
    pp, pap, vv, vav, ww, waw = gram
    sig, tau, rho = shifts
    s0 = pp + EPSILON
    a1 = pap / s0
    pv = pap - sig * pp
    d = sig - a1
    b1s = jnp.maximum(vv + 2.0 * d * pv + d * d * pp, 0.0) / s0 + EPSILON
    b1 = jnp.sqrt(b1s)
    scale = s0 * b1s
    pav = vv + sig * pv
    a2 = (vav + 2.0 * d * pav + d * d * pap) / scale - (pv + d * pp) / s0
    b = tau + d - a2
    a = rho + d * sig - b1s - a2 * d
    pw = vv + (sig - tau) * pv - rho * pp
    vw = vav - tau * vv - rho * pv
    b2s = ww + b * b * vv + a * a * pp + 2.0 * (b * vw + a * pw + a * b * pv)
    b2s = jnp.maximum(b2s, 0.0) / scale + EPSILON
    b2 = jnp.sqrt(b2s)
    vaw = ww + tau * vw + rho * pw
    paw = vw + sig * pw
    top = waw + b * b * vav + a * a * pap + 2.0 * (b * vaw + a * paw + a * b * pav)
    cross = vw + b * vv + a * pv + d * (pw + b * pv + a * pp)
    a3 = top / (scale * b2s) - cross / scale
    return cot[0] * a1 + cot[1] * a2 + cot[2] * a3 + cot[3] * b1 + cot[4] * b2


def swap_rows_lanes(arrays, lane):
    arrays = list(arrays)
    for s in (1, 2, 4, 8):
        low = (lane & s) == 0
        for i in range(16):
            if i & s:
                continue
            one, two = arrays[i], arrays[i + s]
            arrays[i] = jnp.where(low, one, pltpu.roll(two, s, 1))
            arrays[i + s] = jnp.where(low, pltpu.roll(one, 128 - s, 1), two)
    return arrays


def sum_list(parts):
    while len(parts) > 1:
        parts = [parts[i] + parts[i + 1] if i + 1 < len(parts) else parts[i]
                 for i in range(0, len(parts), 2)]
    return parts[0]


def kernel(sizes, *refs):
    probes_ref, kappa_ref, cot_ref, out_ref = refs[:4]
    fields = [refs[4 + i * (LAST + 1) : 4 + (i + 1) * (LAST + 1)] for i in range(GROUPS)]
    (k2, g, products, pv, kv, kt, ov, hz, hr, zs, zm, zp, kz, ars, arr,
     lsem, ssem, rsem, ksem, asem, bsem) = refs[4 + GROUPS * (LAST + 1) :]
    nx, ny, nz = sizes
    gx, gy, gz = lax.axis_index("gx"), lax.axis_index("gy"), lax.axis_index("gz")
    inverse_count = 1.0 / (nx * NX * ny * NY * nz * NZ)

    def load(n):
        return pltpu.make_async_copy((probes_ref, kappa_ref)[n], (pv, kv)[n], lsem.at[n])

    load(0).start()
    load(1).start()

    def when(ok, act):
        if ok is None:
            act()
        else:
            pl.when(ok)(act)

    both = jnp.logical_and
    left, right, down, up = gx > 0, gx < nx - 1, gy > 0, gy < ny - 1
    there = (left, right, down, up, None,
             both(left, down), both(left, up), both(right, down), both(right, up),
             left, right, down, up)
    opposite = (1, 0, 3, 2, 4, 8, 7, 6, 5, 10, 9, 12, 11)
    where_to = (
        lambda: {"gx": gx - 1}, lambda: {"gx": gx + 1}, lambda: {"gy": gy - 1}, lambda: {"gy": gy + 1},
        lambda: {"gz": 1 - gz},
        lambda: {"gx": gx - 1, "gy": gy - 1}, lambda: {"gx": gx - 1, "gy": gy + 1},
        lambda: {"gx": gx + 1, "gy": gy - 1}, lambda: {"gx": gx + 1, "gy": gy + 1},
        lambda: {"gx": gx - 1, "gz": 1 - gz}, lambda: {"gx": gx + 1, "gz": 1 - gz},
        lambda: {"gy": gy - 1, "gz": 1 - gz}, lambda: {"gy": gy + 1, "gz": 1 - gz},
    )

    barrier = pltpu.get_barrier_semaphore()
    group_one = [(i, j) for i in range(nx) for j in range(nz)]

    def greet(where):
        pl.semaphore_signal(barrier, inc=1, device_id=where, device_id_type=MESH)
    greeted = nx * nz - 1 + ny - 1
    for d in (5, 6, 7, 8, 11, 12):
        when(there[d], lambda: greet(where_to[d]()))
        greeted = greeted + there[d].astype(jnp.int32)
    for j in range(ny):
        pl.when(gy != j)(lambda: greet({"gy": j}))
    for i, j in group_one:
        pl.when(jnp.logical_or(gx != i, gz != j))(lambda: greet({"gx": i, "gz": j}))

    lane = lax.broadcasted_iota(jnp.int32, (8, 128), 1)
    sub = lax.broadcasted_iota(jnp.int32, (8, 128), 0)
    lane1 = lax.broadcasted_iota(jnp.int32, (1, 128), 1)
    zero = jnp.zeros((8, 128), jnp.float32)
    first, final = sub == 0, sub == ZL - 1
    zh = lane & (ZH - 1)

    def tile(y, shift=0):
        return pl.ds(TOP + (y + EDGE) * ZL + shift, ZL)

    even = [u for group in fields for u in group[:LAST:2]]

    def clear(cells):
        for u in even:
            for x, y in cells:
                u[x + EDGE, tile(y), :] = zero

    def clear_x(x):
        def one(y, _):
            clear([(x, y), (x + 1, y)])
            return 0
        lax.fori_loop(0, NY, one, 0)

    def clear_y(y):
        def one(x, _):
            clear([(x, y), (x, y + 1)])
            return 0
        lax.fori_loop(0, NX, one, 0)
    pl.when(jnp.logical_not(left))(lambda: clear_x(-2))
    pl.when(jnp.logical_not(right))(lambda: clear_x(NX))
    pl.when(jnp.logical_not(down))(lambda: clear_y(-2))
    pl.when(jnp.logical_not(up))(lambda: clear_y(NY))
    for d, x, y in ((5, -1, -1), (6, -1, NY), (7, NX, -1), (8, NX, NY)):
        pl.when(jnp.logical_not(there[d]))(lambda: clear([(x, y)]))

    load(0).wait()

    def turn_probes(x, _):
        for i in range(GROUPS):
            parts = []
            for p in range(i * GP, (i + 1) * GP):
                parts += [pv[p, x, :, :128], pv[p, x, :, 128:]]
            block = jnp.concatenate(parts, axis=0).T
            rows = swap_rows_lanes([block[j * ZL : j * ZL + ZL, :] for j in range(16)], lane)
            for y in range(NY):
                fields[i][0][x + EDGE, tile(y), :] = rows[y]
        return 0
    lax.fori_loop(0, NX, turn_probes, 0)

    load(1).wait()
    for h in range(2):
        parts = []
        for x in range(h * 4, h * 4 + 4):
            parts += [kv[x, :, :128], kv[x, :, 128:]]
        block = jnp.concatenate(parts, axis=0).T
        rows = swap_rows_lanes([block[j * ZL : j * ZL + ZL, :] for j in range(16)], lane)
        for y in range(NY):
            kt[h, y * ZL : y * ZL + ZL, :] = rows[y] + 6.0

    low2, low1 = (lane & 64) == 0, (lane & 32) == 0

    def spread(y, _):
        for h in range(2):
            row = kt[h, pl.ds(y * ZL, ZL), :]
            turned = pltpu.roll(row, 64, 1)
            for i, two in enumerate((jnp.where(low2, row, turned), jnp.where(low2, turned, row))):
                turned = pltpu.roll(two, 32, 1)
                k2[EDGE + h * 4 + i * 2, tile(y), :] = jnp.where(low1, two, turned)
                k2[EDGE + h * 4 + i * 2 + 1, tile(y), :] = jnp.where(low1, turned, two)
        return 0
    lax.fori_loop(0, NY, spread, 0)

    edge = (ZL - 1) * (1 - gz)
    second = edge + 2 * gz - 1
    edge_lane = (ZH - 1) * (1 - gz)
    slot_x = ((zh * 11) >> 5) - 1
    slot_y = 8 * (zh - 3 * slot_x - 3) + sub - EDGE
    inside_x, inside_y = both(slot_x >= 0, slot_x < NX), both(slot_y >= 0, slot_y < NY)
    inside = both(inside_x, inside_y)

    def packed(u, row):
        out = zero
        for x in range(NX):
            for t in range(2):
                k = 3 * (x + 1) + t
                at = TOP + (EDGE + t * 8) * ZL + row
                moved = pltpu.roll(u[x + EDGE, pl.ds(at, 8, ZL), :], k, 1)
                out = jnp.where(((lane - edge_lane - k) & (ZH - 1)) == 0, moved, out)
        out = jnp.where(gz == 1, out, pltpu.roll(out, 129 - ZH, 1))
        out = pltpu.roll(out, EDGE, 0)
        out = jnp.where(sub < EDGE, pltpu.roll(out, 1, 1), out)
        return jnp.where(inside, out, 0.0)

    def copy(i, f, d):
        if f < 0:
            u, width, r, zsrc, zdst = k2, 1, None, kz.at[0], kz.at[1]
            sems = (ksem.at[0, d], ksem.at[1, d])
        else:
            r = f // 2
            u, width, zsrc, zdst = fields[i][f], 1 if f == LAST - 1 else 2, zs.at[i, r], hz.at[i, r]
            sems = (ssem.at[i, r, d], rsem.at[i, r, d])
        own_x, own_y = pl.ds(EDGE, NX), pl.ds(TOP + EDGE * ZL, NY * ZL)

        def xs(x):
            return pl.ds(x + EDGE, width)

        def ys(y):
            return pl.ds(TOP + (y + EDGE) * ZL, width * ZL)
        if d == 0:
            src, dst = u.at[xs(0), own_y], u.at[xs(NX), own_y]
        elif d == 1:
            src, dst = u.at[xs(NX - width), own_y], u.at[xs(-width), own_y]
        elif d == 2:
            src, dst = u.at[own_x, ys(0)], u.at[own_x, ys(NY)]
        elif d == 3:
            src, dst = u.at[own_x, ys(NY - width)], u.at[own_x, ys(-width)]
        elif d == 4:
            src, dst = zsrc, zdst
        elif d < 9:
            x, y = (0, NX - 1)[(d - 5) // 2], (0, NY - 1)[(d - 5) % 2]
            tx, ty = (NX, -1)[(d - 5) // 2], (NY, -1)[(d - 5) % 2]
            src, dst = u.at[x + EDGE, tile(y)], u.at[tx + EDGE, tile(ty)]
        else:
            src, dst = zs.at[i, r, 0], hr.at[i, r, opposite[d] - 9]
        return pltpu.make_async_remote_copy(
            src, dst, sems[0], sems[1], device_id=where_to[d](), device_id_type=MESH)

    def directions(f):
        return range(5) if f < 0 or f == LAST - 1 else range(13)

    def send(i, f):
        ds = directions(f)
        for d in (*range(5, 9), 2, 3):
            if d in ds:
                when(there[d], lambda: copy(i, f, d).start())
        if f < 0:
            kz[0] = packed(k2, edge)
        else:
            zs[i, f // 2, 0] = packed(fields[i][f], edge)
            if f < LAST - 1:
                zs[i, f // 2, 1] = packed(fields[i][f], second)
        for d in (4, *range(9, 13), 0, 1):
            if d in ds:
                when(there[d], lambda: copy(i, f, d).start())

    def receive(i, f):
        for d in directions(f):
            when(there[d], lambda: copy(i, f, opposite[d]).wait_recv())

    edge_low, edge_high = zh == 0, zh == ZH - 1

    def carry_z(u, layer, xs):
        layer = jnp.where(gz == 0, pltpu.roll(layer, ZH - 1, 1), layer)
        under_edge, over_edge = gz == 1, gz == 0
        for x in xs:
            for t in range(3):
                k = 3 * (x + 1) + t
                at = TOP + t * 8 * ZL
                halo = pltpu.roll(layer, 128 - k, 1) if k else layer
                high = pltpu.roll(u[x + EDGE, pl.ds(at + ZL - 1, 8, ZL), :], 1, 1)
                low = pltpu.roll(u[x + EDGE, pl.ds(at, 8, ZL), :], 127, 1)
                zm[x + 1, t * 8 : t * 8 + 8, :] = jnp.where(
                    edge_low, jnp.where(under_edge, halo, 0.0), high)
                zp[x + 1, t * 8 + 8 : t * 8 + 16, :] = jnp.where(
                    edge_high, jnp.where(over_edge, halo, 0.0), low)

    def main(u, v, ext):
        xs = list(range(-1, NX + 1)) if ext else list(range(NX))

        def row(y, xs, below, here, above, ok=None):
            done = []
            for x in xs:
                under = jnp.where(first, zm[x + 1, pl.ds(y + EDGE, 8), :], u[x + EDGE, tile(y, -1), :])
                over = jnp.where(final, zp[x + 1, pl.ds(y + EDGE + 1, 8), :], u[x + EDGE, tile(y, 1), :])
                total = (under + over) + (below[x] + above[x]) + (here[x - 1] + here[x + 1])
                value = k2[x + EDGE, tile(y), :] * here[x] - total
                if x in (-1, NX):
                    value = jnp.where(left if x < 0 else right, value, 0.0)
                if ok is not None:
                    value = jnp.where(ok, value, 0.0)
                done.append(value)
            for x, value in zip(xs, done):
                v[x + EDGE, tile(y), :] = value

        def read(y, xs):
            return {x: u[x + EDGE, tile(y), :] for x in xs}
        wide = [xs[0] - 1, *xs, xs[-1] + 1]
        if ext:
            for y, ok in ((-1, down), (NY, up)):
                own = list(range(NX))
                row(y, own, read(y - 1, own), read(y, xs), read(y + 1, own), ok)

        def pair(q, carry):
            below, here = dict(zip(xs, carry[: len(xs)])), dict(zip(wide, carry[len(xs) :]))
            for y in (2 * q, 2 * q + 1):
                above = read(y + 1, wide)
                row(y, xs, below, here, above)
                below, here = {x: here[x] for x in xs}, above
            return tuple(below[x] for x in xs) + tuple(here[x] for x in wide)
        below, here = read(-1, xs), read(0, wide)
        lax.fori_loop(
            0, NY // 2, pair, tuple(below[x] for x in xs) + tuple(here[x] for x in wide))

    def slot(i, f):
        u = fields[i][f]
        r = f // 2
        receive(i, f)
        if f == LAST - 1:
            carry_z(u, hz[i, r, 0], range(NX))
            main(u, fields[i][f + 1], False)
            return
        layer = hz[i, r, 0]
        for d, place, turn in ((0, both(slot_x == -1, inside_y), 128 - 3 * NX),
                               (1, both(slot_x == NX, inside_y), 3 * NX),
                               (2, both(slot_y == -1, inside_x), 126),
                               (3, both(slot_y == NY, inside_x), 2)):
            ring = pltpu.roll(hr[i, r, d], turn, 1)
            layer = jnp.where(both(place, there[d]), ring, layer)
        carry_z(u, layer, range(-1, NX + 1))
        main(u, fields[i][f + 1], True)
        ahead, behind = pltpu.roll(layer, 7, 0), pltpu.roll(layer, 1, 0)
        ahead = jnp.where(final, pltpu.roll(ahead, 127, 1), ahead)
        behind = jnp.where(first, pltpu.roll(behind, 1, 1), behind)
        total = (ahead + behind) + (pltpu.roll(layer, 3, 1) + pltpu.roll(layer, 125, 1))
        total = total + (hz[i, r, 1] + zs[i, r, 0])
        layer = jnp.where(inside, kz[1] * layer - total, 0.0)
        carry_z(fields[i][f + 1], layer, range(NX))
        main(fields[i][f + 1], fields[i][f + 2], False)
        send(i, f + 2)

    def phase_peers(n):
        if n % 2 == 0:
            return [(jnp.logical_or(gx != i, gz != j), i * nz + j, {"gx": i, "gz": j})
                    for i, j in group_one], gx * nz + gz
        return [(gy != j, j, {"gy": j}) for j in range(ny)], gy

    def phase_start(n, value):
        ars[n] = value
        peers, me = phase_peers(n)
        for ok, slot, where in peers:
            pl.when(ok)(lambda: pltpu.make_async_remote_copy(
                ars.at[n], arr.at[n, me], asem.at[n, slot], bsem.at[n, me],
                device_id=where, device_id_type=MESH).start())

    def phase_wait(n, act):
        peers, me = phase_peers(n)
        for ok, slot, where in peers:
            pl.when(ok)(lambda: act(pltpu.make_async_remote_copy(
                ars.at[n], arr.at[n, slot], asem.at[n, slot], bsem.at[n, slot],
                device_id=where, device_id_type=MESH)))
        return peers, me

    def phase_end(n):
        peers, me = phase_wait(n, lambda c: c.wait_recv())
        arr[n, me] = ars[n]
        return sum_list([arr[n, i] for i in range(len(peers))])

    def stack(rows):
        out = zero
        for i, row in enumerate(rows):
            out = jnp.where(sub == i, jnp.sum(row, axis=0, keepdims=True), out)
        return out

    def over_lanes(value):
        for s in (1, 2, 4, 8, 16):
            low = (lane & s) == 0
            value = value + jnp.where(low, pltpu.roll(value, 128 - s, 1), pltpu.roll(value, s, 1))
        return value * inverse_count

    inner = both(sub > 0, sub < ZL - 1)
    early = []
    for i in range(GROUPS):
        u = fields[i][0]

        def whole(y, acc):
            return acc + sum_list([u[x + EDGE, tile(y), :] * u[x + EDGE, tile(y), :] for x in range(NX)])

        def core(y, acc):
            here = [u[x + EDGE, tile(y), :] for x in range(NX)]
            zeroth, next_ = acc
            for x in range(1, NX - 1):
                total = u[x + EDGE, tile(y - 1), :] + u[x + EDGE, tile(y + 1), :]
                total = total + (u[x + EDGE, tile(y, -1), :] + u[x + EDGE, tile(y, 1), :])
                total = total + (here[x - 1] + here[x + 1])
                value = jnp.where(inner, k2[x + EDGE, tile(y), :] * here[x] - total, 0.0)
                mine = jnp.where(inner, here[x], 0.0)
                zeroth, next_ = zeroth + mine * mine, next_ + value * value
            return zeroth, next_
        early.append(lax.fori_loop(0, NY, whole, zero))
        early += list(lax.fori_loop(1, NY - 1, core, (zero, zero)))
    early = jnp.concatenate([stack(early), zero], axis=0)

    pl.semaphore_wait(barrier, greeted)
    send(0, 0)
    send(0, -2)
    send(1, 0)
    phase_start(0, early)
    receive(0, -2)
    slot(0, 0)
    slot(1, 0)
    phase_start(1, phase_end(0))
    slot(0, 2)
    slot(1, 2)
    slot(0, 4)

    raw = over_lanes(phase_end(1)[0:8])
    norms, shifts = [], []
    for i in range(GROUPS):
        m0, i0, i1 = (raw[3 * i + j : 3 * i + j + 1] for j in range(3))
        tau = jnp.clip(i1 / jnp.maximum(i0, 1e-30), 0.0, 256.0)
        norms.append(m0)
        shifts.append((tau * m0 / (m0 + EPSILON), tau))

    def refine(i):
        sig, tau = shifts[i]
        e1, e0 = -(sig + tau), sig * tau

        def one(y, acc):
            au, av, akv, aw, akw = acc
            for x in range(NX):
                t = [fields[i][j][x + EDGE, tile(y), :] for j in range(6)]
                v = t[2] - sig * t[0]
                kv_ = t[3] - sig * t[1]
                w = (t[4] + e1 * t[2]) + e0 * t[0]
                kw = (t[5] + e1 * t[3]) + e0 * t[1]
                au, av, akv = au + t[1] * t[1], av + v * v, akv + kv_ * kv_
                aw, akw = aw + w * w, akw + kw * kw
            return au, av, akv, aw, akw
        return lax.fori_loop(0, NY, one, (zero,) * 5)

    low = refine(0)
    slot(1, 4)
    high = refine(1)
    phase_start(2, jnp.concatenate([stack(low), stack(high)], axis=0))
    slot(0, 6)
    slot(1, 6)
    phase_start(3, phase_end(2))
    slot(0, 8)
    slot(1, 8)

    def part(y, _):
        for i in range(GROUPS):
            for x in range(NX):
                t = [fields[i][j][x + EDGE, tile(y), :] for j in range(LAST + 1)]
                for k in range(1, 6):
                    products[i, k - 1, x, pl.ds(y * ZL, ZL), :] = sum_list(
                        [t[j] * t[2 * k - 1 - j] for j in range(k)])
        return 0
    lax.fori_loop(0, NY, part, 0)

    fine = phase_end(3)
    fine = [over_lanes(fine[0:8]), over_lanes(fine[8:16])]
    weights = []
    for i in range(GROUPS):
        cot = []
        for j in range(5):
            row = jnp.zeros((1, 128), jnp.float32)
            for p in range(GP):
                row = jnp.where((lane1 >> 5) == p, cot_ref[j, i * GP + p], row)
            cot.append(row)
        sig, tau = shifts[i]
        e1, e0 = -(sig + tau), sig * tau
        gram = (norms[i],) + tuple(fine[i][j : j + 1] for j in range(5))
        _, back = jax.vjp(lambda *q: scalars(q, (sig, tau, jnp.zeros_like(sig)), cot), *gram)
        _, gpap, gvv, gvav, gww, gwaw = back(jnp.ones((1, 128), jnp.float32))
        sq = e1 * e1 + 2.0 * e0
        weights.append([jnp.broadcast_to(2.0 * c, (ZL, 128)) for c in (
            gpap - 2.0 * sig * gvv + sig * sig * gvav + 2.0 * e1 * e0 * gww + e0 * e0 * gwaw,
            gvv - 2.0 * sig * gvav + sq * gww + 2.0 * e1 * e0 * gwaw,
            gvav + 2.0 * e1 * gww + sq * gwaw,
            gww + 2.0 * e1 * gwaw,
            gwaw,
        )])

    def gather(y, _):
        at = pl.ds(y * ZL, ZL)
        for h in range(2):
            t = [sum_list([weights[i][k] * products[i, k, h * 4 + x, at, :]
                           for i in range(GROUPS) for k in range(5)]) for x in range(4)]
            t = [jnp.where(low2, t[j], t[j + 2])
                 + pltpu.roll(jnp.where(low2, t[j + 2], t[j]), 64, 1) for j in range(2)]
            g[h, at, :] = jnp.where(
                low1, t[0] + pltpu.roll(t[0], 96, 1), t[1] + pltpu.roll(t[1], 32, 1))
        return 0
    lax.fori_loop(0, NY, gather, 0, unroll=True)
    for h in range(2):
        rows = swap_rows_lanes([g[h, y * ZL : y * ZL + ZL, :] for y in range(NY)], lane)
        block = jnp.concatenate(rows, axis=0).T
        for x in range(4):
            for half in range(2):
                at = x * 32 + half * 16
                ov[h * 4 + x, :, half * 128 : half * 128 + 128] = block[at : at + 16, :]
    store = pltpu.make_async_copy(ov, out_ref, lsem.at[2])
    store.start()

    for i, f in [(0, -2)] + [(i, f) for f in range(0, LAST, 2) for i in range(GROUPS)]:
        for d in directions(f):
            when(there[d], lambda: copy(i, f, d).wait_send())
    for n in range(4):
        phase_wait(n, lambda c: c.wait_send())
    store.wait()


def body(probes, kappa2, cotangents):
    sizes = tuple(lax.axis_size(a) for a in ("gx", "gy", "gz"))
    f32 = jnp.float32
    any_space = pl.BlockSpec(memory_space=pl.ANY)
    rounds = (LAST + 1) // 2
    return pl.pallas_call(
        functools.partial(kernel, sizes),
        out_shape=jax.ShapeDtypeStruct((NX, NY, NZ), f32),
        in_specs=[any_space, any_space, pl.BlockSpec(memory_space=pltpu.SMEM)],
        out_specs=any_space,
        scratch_shapes=[
            *[pltpu.VMEM((SLABS, ROWS, 128), f32) for _ in range(GROUPS * (LAST + 1))],
            pltpu.VMEM((SLABS, ROWS, 128), f32),
            pltpu.VMEM((2, NY * ZL, 128), f32),
            pltpu.VMEM((GROUPS, 5, NX, NY * ZL, 128), f32),
            pltpu.VMEM((NP, NX, NY, NZ), f32),
            pltpu.VMEM((NX, NY, NZ), f32),
            pltpu.VMEM((2, NY * ZL, 128), f32),
            pltpu.VMEM((NX, NY, NZ), f32),
            pltpu.VMEM((GROUPS, rounds, 2, 8, 128), f32),
            pltpu.VMEM((GROUPS, rounds, 4, 8, 128), f32),
            pltpu.VMEM((GROUPS, rounds, 2, 8, 128), f32),
            pltpu.VMEM((NX + 2, TILES + 8, 128), f32),
            pltpu.VMEM((NX + 2, TILES + 8, 128), f32),
            pltpu.VMEM((2, 8, 128), f32),
            pltpu.VMEM((4, 16, 128), f32),
            pltpu.VMEM((4, 16, 16, 128), f32),
            pltpu.SemaphoreType.DMA((3,)),
            pltpu.SemaphoreType.DMA((GROUPS, rounds, 13)),
            pltpu.SemaphoreType.DMA((GROUPS, rounds, 13)),
            pltpu.SemaphoreType.DMA((2, 5)),
            pltpu.SemaphoreType.DMA((4, 16)),
            pltpu.SemaphoreType.DMA((4, 16)),
        ],
        compiler_params=pltpu.CompilerParams(
            collective_id=0, has_side_effects=True, vmem_limit_bytes=63 << 20
        ),
    )(probes, kappa2, cotangents)


def solution(mesh):
    return jax.shard_map(
        body,
        mesh=mesh,
        in_specs=(P(None, "gx", "gy", "gz"), P("gx", "gy", "gz"), P()),
        out_specs=P("gx", "gy", "gz"),
        check_vma=False,
    )
```

```python
import functools

import jax
import jax.numpy as jnp
from jax import lax
from jax.experimental import pallas as pl
from jax.experimental.pallas import tpu as pltpu
from jax.sharding import PartitionSpec as P

EPSILON = 1e-06
MESH = pl.DeviceIdType.MESH
NP, NX, NY, NZ = 8, 8, 16, 256
GROUPS, GP = 2, 4
ZL, ZH = 8, 32
TOP = 8
EDGE = 3
SLABS, TILES = NX + 2 * EDGE, 24
ROWS = TOP + TILES * ZL + 8
LAST = 9


def scalars(gram, shifts, cot):
    pp, pap, vv, vav, ww, waw = gram
    sig, tau, rho = shifts
    s0 = pp + EPSILON
    a1 = pap / s0
    pv = pap - sig * pp
    d = sig - a1
    b1s = jnp.maximum(vv + 2.0 * d * pv + d * d * pp, 0.0) / s0 + EPSILON
    b1 = jnp.sqrt(b1s)
    scale = s0 * b1s
    pav = vv + sig * pv
    a2 = (vav + 2.0 * d * pav + d * d * pap) / scale - (pv + d * pp) / s0
    b = tau + d - a2
    a = rho + d * sig - b1s - a2 * d
    pw = vv + (sig - tau) * pv - rho * pp
    vw = vav - tau * vv - rho * pv
    b2s = ww + b * b * vv + a * a * pp + 2.0 * (b * vw + a * pw + a * b * pv)
    b2s = jnp.maximum(b2s, 0.0) / scale + EPSILON
    b2 = jnp.sqrt(b2s)
    vaw = ww + tau * vw + rho * pw
    paw = vw + sig * pw
    top = waw + b * b * vav + a * a * pap + 2.0 * (b * vaw + a * paw + a * b * pav)
    cross = vw + b * vv + a * pv + d * (pw + b * pv + a * pp)
    a3 = top / (scale * b2s) - cross / scale
    return cot[0] * a1 + cot[1] * a2 + cot[2] * a3 + cot[3] * b1 + cot[4] * b2


def swap_rows_lanes(arrays, lane):
    arrays = list(arrays)
    for s in (1, 2, 4, 8):
        low = (lane & s) == 0
        for i in range(16):
            if i & s:
                continue
            one, two = arrays[i], arrays[i + s]
            arrays[i] = jnp.where(low, one, pltpu.roll(two, s, 1))
            arrays[i + s] = jnp.where(low, pltpu.roll(one, 128 - s, 1), two)
    return arrays


def sum_list(parts):
    while len(parts) > 1:
        parts = [parts[i] + parts[i + 1] if i + 1 < len(parts) else parts[i]
                 for i in range(0, len(parts), 2)]
    return parts[0]


def kernel(sizes, *refs):
    probes_ref, kappa_ref, cot_ref, out_ref = refs[:4]
    fields = [refs[4 + i * (LAST + 1) : 4 + (i + 1) * (LAST + 1)] for i in range(GROUPS)]
    (k2, g, products, pv, kv, kt, ov, hz, hr, hc, zs, zm, zp, kz, kr, ars, arr,
     lsem, ssem, rsem, ksem, asem, bsem) = refs[4 + GROUPS * (LAST + 1) :]
    nx, ny, nz = sizes
    gx, gy, gz = lax.axis_index("gx"), lax.axis_index("gy"), lax.axis_index("gz")
    inverse_count = 1.0 / (nx * NX * ny * NY * nz * NZ)

    def load(n):
        return pltpu.make_async_copy((probes_ref, kappa_ref)[n], (pv, kv)[n], lsem.at[n])

    load(0).start()
    load(1).start()

    def when(ok, act):
        if ok is None:
            act()
        else:
            pl.when(ok)(act)

    both = jnp.logical_and
    left, right, down, up = gx > 0, gx < nx - 1, gy > 0, gy < ny - 1
    there = (left, right, down, up, None,
             both(left, down), both(left, up), both(right, down), both(right, up),
             left, right, down, up,
             both(left, down), both(left, up), both(right, down), both(right, up))
    opposite = (1, 0, 3, 2, 4, 8, 7, 6, 5, 10, 9, 12, 11, 16, 15, 14, 13)
    where_to = (
        lambda: {"gx": gx - 1}, lambda: {"gx": gx + 1}, lambda: {"gy": gy - 1}, lambda: {"gy": gy + 1},
        lambda: {"gz": 1 - gz},
        lambda: {"gx": gx - 1, "gy": gy - 1}, lambda: {"gx": gx - 1, "gy": gy + 1},
        lambda: {"gx": gx + 1, "gy": gy - 1}, lambda: {"gx": gx + 1, "gy": gy + 1},
        lambda: {"gx": gx - 1, "gz": 1 - gz}, lambda: {"gx": gx + 1, "gz": 1 - gz},
        lambda: {"gy": gy - 1, "gz": 1 - gz}, lambda: {"gy": gy + 1, "gz": 1 - gz},
        lambda: {"gx": gx - 1, "gy": gy - 1, "gz": 1 - gz}, lambda: {"gx": gx - 1, "gy": gy + 1, "gz": 1 - gz},
        lambda: {"gx": gx + 1, "gy": gy - 1, "gz": 1 - gz}, lambda: {"gx": gx + 1, "gy": gy + 1, "gz": 1 - gz},
    )

    barrier = pltpu.get_barrier_semaphore()
    group_one = [(i, j) for i in range(nx) for j in range(nz)]

    def greet(where):
        pl.semaphore_signal(barrier, inc=1, device_id=where, device_id_type=MESH)
    greeted = nx * nz - 1 + ny - 1
    for d in (5, 6, 7, 8, 11, 12, 13, 14, 15, 16):
        when(there[d], lambda: greet(where_to[d]()))
        greeted = greeted + there[d].astype(jnp.int32)
    for j in range(ny):
        pl.when(gy != j)(lambda: greet({"gy": j}))
    for i, j in group_one:
        pl.when(jnp.logical_or(gx != i, gz != j))(lambda: greet({"gx": i, "gz": j}))

    lane = lax.broadcasted_iota(jnp.int32, (8, 128), 1)
    sub = lax.broadcasted_iota(jnp.int32, (8, 128), 0)
    lane1 = lax.broadcasted_iota(jnp.int32, (1, 128), 1)
    zero = jnp.zeros((8, 128), jnp.float32)
    first, final = sub == 0, sub == ZL - 1
    zh = lane & (ZH - 1)

    def tile(y, shift=0):
        return pl.ds(TOP + (y + EDGE) * ZL + shift, ZL)

    sent = [u for group in fields for u in group[: LAST : EDGE]]

    def clear(x, y):
        for u in sent:
            u[x + EDGE, tile(y), :] = zero

    def clear_x(x):
        def one(y, _):
            for j in range(EDGE):
                clear(x + j, y)
            return 0
        lax.fori_loop(0, NY, one, 0)

    def clear_y(y):
        def one(x, _):
            for j in range(EDGE):
                clear(x, y + j)
            return 0
        lax.fori_loop(0, NX, one, 0)

    def clear_corner(x, y):
        for j in range(2):
            for k in range(2):
                clear(x + j, y + k)
    pl.when(jnp.logical_not(left))(lambda: clear_x(-EDGE))
    pl.when(jnp.logical_not(right))(lambda: clear_x(NX))
    pl.when(jnp.logical_not(down))(lambda: clear_y(-EDGE))
    pl.when(jnp.logical_not(up))(lambda: clear_y(NY))
    for d, x, y in ((5, -2, -2), (6, -2, NY), (7, NX, -2), (8, NX, NY)):
        pl.when(jnp.logical_not(there[d]))(lambda: clear_corner(x, y))

    load(0).wait()

    def turn_probes(x, _):
        for i in range(GROUPS):
            parts = []
            for p in range(i * GP, (i + 1) * GP):
                parts += [pv[p, x, :, :128], pv[p, x, :, 128:]]
            block = jnp.concatenate(parts, axis=0).T
            rows = swap_rows_lanes([block[j * ZL : j * ZL + ZL, :] for j in range(16)], lane)
            for y in range(NY):
                fields[i][0][x + EDGE, tile(y), :] = rows[y]
        return 0
    lax.fori_loop(0, NX, turn_probes, 0)

    load(1).wait()
    for h in range(2):
        parts = []
        for x in range(h * 4, h * 4 + 4):
            parts += [kv[x, :, :128], kv[x, :, 128:]]
        block = jnp.concatenate(parts, axis=0).T
        rows = swap_rows_lanes([block[j * ZL : j * ZL + ZL, :] for j in range(16)], lane)
        for y in range(NY):
            kt[h, y * ZL : y * ZL + ZL, :] = rows[y] + 6.0

    low2, low1 = (lane & 64) == 0, (lane & 32) == 0

    def spread(y, _):
        for h in range(2):
            row = kt[h, pl.ds(y * ZL, ZL), :]
            turned = pltpu.roll(row, 64, 1)
            for i, two in enumerate((jnp.where(low2, row, turned), jnp.where(low2, turned, row))):
                turned = pltpu.roll(two, 32, 1)
                k2[EDGE + h * 4 + i * 2, tile(y), :] = jnp.where(low1, two, turned)
                k2[EDGE + h * 4 + i * 2 + 1, tile(y), :] = jnp.where(low1, turned, two)
        return 0
    lax.fori_loop(0, NY, spread, 0)

    edge = (ZL - 1) * (1 - gz)
    inward = 2 * gz - 1
    edge_lane = (ZH - 1) * (1 - gz)
    slot_x = ((zh * 11) >> 5) - 1
    slot_y = 8 * (zh - 3 * slot_x - 3) + sub - EDGE
    inside_x, inside_y = both(slot_x >= 0, slot_x < NX), both(slot_y >= 0, slot_y < NY)
    inside = both(inside_x, inside_y)
    beside = (both(slot_x == -1, inside_y), both(slot_x == NX, inside_y),
              both(slot_y == -1, inside_x), both(slot_y == NY, inside_x))
    near = inside
    for d in range(4):
        near = jnp.logical_or(near, both(beside[d], there[d]))

    def packed(u, row):
        out = zero
        for x in range(NX):
            for t in range(2):
                k = 3 * (x + 1) + t
                at = TOP + (EDGE + t * 8) * ZL + row
                moved = pltpu.roll(u[x + EDGE, pl.ds(at, 8, ZL), :], k, 1)
                out = jnp.where(((lane - edge_lane - k) & (ZH - 1)) == 0, moved, out)
        out = jnp.where(gz == 1, out, pltpu.roll(out, 129 - ZH, 1))
        out = pltpu.roll(out, EDGE, 0)
        out = jnp.where(sub < EDGE, pltpu.roll(out, 1, 1), out)
        return jnp.where(inside, out, 0.0)

    def packed_near(u):
        out = zero
        for x in range(-1, NX + 1):
            for t in range(3):
                k = 3 * (x + 1) + t
                row = u[x + EDGE, pl.ds(TOP + t * 8 * ZL + edge, 8, ZL), :]
                moved = pltpu.roll(row, k, 1) if k else row
                out = jnp.where(((lane - edge_lane - k) & (ZH - 1)) == 0, moved, out)
        out = jnp.where(gz == 1, out, pltpu.roll(out, 129 - ZH, 1))
        return jnp.where(near, out, 0.0)

    def copy(i, f, d):
        if f < 0:
            u, width, zsrc, zdst, ring = k2, EDGE - 1, kz.at[0], kz.at[1], kr
            sems = (ksem.at[0, d], ksem.at[1, d])
        else:
            r = f // EDGE
            u, width, zsrc, zdst, ring = fields[i][f], EDGE, zs.at[i, r], hz.at[i, r], hr.at[i, r]
            sems = (ssem.at[i, r, d], rsem.at[i, r, d])
        own_x, own_y = pl.ds(EDGE, NX), pl.ds(TOP + EDGE * ZL, NY * ZL)

        def xs(x):
            return pl.ds(x + EDGE, width)

        def ys(y):
            return pl.ds(TOP + (y + EDGE) * ZL, width * ZL)
        if d == 0:
            src, dst = u.at[xs(0), own_y], u.at[xs(NX), own_y]
        elif d == 1:
            src, dst = u.at[xs(NX - width), own_y], u.at[xs(-width), own_y]
        elif d == 2:
            src, dst = u.at[own_x, ys(0)], u.at[own_x, ys(NY)]
        elif d == 3:
            src, dst = u.at[own_x, ys(NY - width)], u.at[own_x, ys(-width)]
        elif d == 4:
            src, dst = zsrc, zdst
        elif d < 9:
            x, y = (0, NX - 2)[(d - 5) // 2], (0, NY - 2)[(d - 5) % 2]
            tx, ty = (NX, -2)[(d - 5) // 2], (NY, -2)[(d - 5) % 2]
            src, dst = (u.at[pl.ds(p + EDGE, 2), pl.ds(TOP + (q + EDGE) * ZL, 2 * ZL)]
                        for p, q in ((x, y), (tx, ty)))
        elif d < 13:
            src, dst = zsrc.at[pl.ds(0, 2)], ring.at[opposite[d] - 9]
        else:
            src, dst = zsrc.at[0], hc.at[i, r, opposite[d] - 13]
        return pltpu.make_async_remote_copy(
            src, dst, sems[0], sems[1], device_id=where_to[d](), device_id_type=MESH)

    def directions(f):
        return range(13) if f < 0 else range(17)

    def send(i, f):
        ds = directions(f)
        for d in (*range(5, 9), 2, 3):
            if d in ds:
                when(there[d], lambda: copy(i, f, d).start())
        for j in range(EDGE):
            if f < 0:
                kz[0, j] = packed(k2, edge + j * inward)
            else:
                zs[i, f // EDGE, j] = packed(fields[i][f], edge + j * inward)
        for d in (*range(13, 17), *range(9, 13), 4, 0, 1):
            if d in ds:
                when(there[d], lambda: copy(i, f, d).start())

    def receive(i, f):
        for d in directions(f):
            when(there[d], lambda: copy(i, f, opposite[d]).wait_recv())

    edge_low, edge_high = zh == 0, zh == ZH - 1

    def carry_z(u, layer, xs, far=None):
        def aligned(value):
            return jnp.where(gz == 0, pltpu.roll(value, ZH - 1, 1), value)
        layer = aligned(layer)
        if far is not None:
            far = aligned(far)
        under_edge, over_edge = gz == 1, gz == 0
        for x in xs:
            for t in range(3):
                k = 3 * (min(max(x, -1), NX) + 1) + t
                at = TOP + t * 8 * ZL
                halo = layer if -1 <= x <= NX else far
                halo = pltpu.roll(halo, 128 - k, 1) if k else halo
                high = pltpu.roll(u[x + EDGE, pl.ds(at + ZL - 1, 8, ZL), :], 1, 1)
                low = pltpu.roll(u[x + EDGE, pl.ds(at, 8, ZL), :], 127, 1)
                zm[x + 2, t * 8 : t * 8 + 8, :] = jnp.where(
                    edge_low, jnp.where(under_edge, halo, 0.0), high)
                zp[x + 2, t * 8 + 8 : t * 8 + 16, :] = jnp.where(
                    edge_high, jnp.where(over_edge, halo, 0.0), low)

    def main(u, v, ext):
        xs = list(range(-ext, NX + ext))

        def row(y, xs, below, here, above, ok=None):
            done = []
            for x in xs:
                under = jnp.where(first, zm[x + 2, pl.ds(y + EDGE, 8), :], u[x + EDGE, tile(y, -1), :])
                over = jnp.where(final, zp[x + 2, pl.ds(y + EDGE + 1, 8), :], u[x + EDGE, tile(y, 1), :])
                total = (under + over) + (below[x] + above[x]) + (here[x - 1] + here[x + 1])
                value = k2[x + EDGE, tile(y), :] * here[x] - total
                if not 0 <= x < NX:
                    value = jnp.where(left if x < 0 else right, value, 0.0)
                if ok is not None:
                    value = jnp.where(ok, value, 0.0)
                done.append(value)
            for x, value in zip(xs, done):
                v[x + EDGE, tile(y), :] = value

        def read(y, xs):
            return {x: u[x + EDGE, tile(y), :] for x in xs}
        wide = [xs[0] - 1, *xs, xs[-1] + 1]
        for j in range(1, ext + 1):
            for y, ok in ((-j, down), (NY - 1 + j, up)):
                some = list(range(j - ext, NX + ext - j))
                row(y, some, read(y - 1, some), read(y, [some[0] - 1, *some, some[-1] + 1]),
                    read(y + 1, some), ok)

        def pair(q, carry):
            below, here = dict(zip(xs, carry[: len(xs)])), dict(zip(wide, carry[len(xs) :]))
            for y in (2 * q, 2 * q + 1):
                above = read(y + 1, wide)
                row(y, xs, below, here, above)
                below, here = {x: here[x] for x in xs}, above
            return tuple(below[x] for x in xs) + tuple(here[x] for x in wide)
        below, here = read(-1, xs), read(0, wide)
        lax.fori_loop(
            0, NY // 2, pair, tuple(below[x] for x in xs) + tuple(here[x] for x in wide))

    def z_step(here, over, under, kappa, far=None):
        ahead, behind = pltpu.roll(here, 7, 0), pltpu.roll(here, 1, 0)
        ahead = jnp.where(final, pltpu.roll(ahead, 127, 1), ahead)
        behind = jnp.where(first, pltpu.roll(behind, 1, 1), behind)
        lower, higher = pltpu.roll(here, 3, 1), pltpu.roll(here, 125, 1)
        if far is not None:
            lower, higher = jnp.where(slot_x == -1, far, lower), jnp.where(slot_x == NX, far, higher)
        return kappa * here - ((ahead + behind) + (lower + higher) + (over + under))

    def ringed(base, rings, depth):
        for d, turn in ((0, 128 - 3 * NX), (1, 3 * NX), (2, 126), (3, 2)):
            place = beside[d]
            if depth == 2 and d == 2:
                place = both(both(slot_y < 0, slot_y > -3), inside_x)
            elif depth == 2 and d == 3:
                place = both(both(slot_y >= NY, slot_y < NY + 2), inside_x)
            base = jnp.where(both(place, there[d]), pltpu.roll(rings[d], turn, 1), base)
        return base

    def slot(i, f, between=None):
        r = f // EDGE
        u = fields[i][f : f + EDGE + 1]
        receive(i, f)
        layer = ringed(hz[i, r, 0], [hr[i, r, d, 0] for d in range(4)], 2)
        for d, x, y, turn in ((0, -1, -1, -3 * NX - 2), (1, -1, NY, -3 * NX + 2),
                              (2, NX, -1, 3 * NX - 2), (3, NX, NY, 3 * NX + 2)):
            place = both(both(slot_x == x, slot_y == y), there[13 + d])
            layer = jnp.where(place, pltpu.roll(hc[i, r, d], turn % 128, 1), layer)
        far = jnp.where(both(beside[0], left), pltpu.roll(hr[i, r, 0, 0], 128 - 3 * (NX - 1), 1), 0.0)
        far = jnp.where(both(beside[1], right), pltpu.roll(hr[i, r, 1, 0], 3 * (NX - 1), 1), far)
        next_ = ringed(hz[i, r, 1], [hr[i, r, d, 1] for d in range(4)], 1)
        carry_z(u[0], layer, range(-2, NX + 2), far)
        main(u[0], u[1], 2)
        one = jnp.where(near, z_step(layer, next_, packed_near(u[0]), kappa_near, far), 0.0)
        two = jnp.where(inside, z_step(next_, hz[i, r, 2], layer, kz[1, 1]), 0.0)
        carry_z(u[1], one, range(-1, NX + 1))
        main(u[1], u[2], 1)
        if between is not None:
            between()
        one = jnp.where(inside, z_step(one, two, packed(u[1], edge), kz[1, 0]), 0.0)
        carry_z(u[2], one, range(NX))
        main(u[2], u[3], 0)
        if f + EDGE < LAST:
            send(i, f + EDGE)

    def phase_peers(n):
        if n % 2 == 0:
            return [(jnp.logical_or(gx != i, gz != j), i * nz + j, {"gx": i, "gz": j})
                    for i, j in group_one], gx * nz + gz
        return [(gy != j, j, {"gy": j}) for j in range(ny)], gy

    def phase_start(n, value):
        ars[n] = value
        peers, me = phase_peers(n)
        for ok, slot, where in peers:
            pl.when(ok)(lambda: pltpu.make_async_remote_copy(
                ars.at[n], arr.at[n, me], asem.at[n, slot], bsem.at[n, me],
                device_id=where, device_id_type=MESH).start())

    def phase_wait(n, act):
        peers, me = phase_peers(n)
        for ok, slot, where in peers:
            pl.when(ok)(lambda: act(pltpu.make_async_remote_copy(
                ars.at[n], arr.at[n, slot], asem.at[n, slot], bsem.at[n, slot],
                device_id=where, device_id_type=MESH)))
        return peers, me

    def phase_end(n):
        peers, me = phase_wait(n, lambda c: c.wait_recv())
        arr[n, me] = ars[n]
        return sum_list([arr[n, i] for i in range(len(peers))])

    def stack(rows):
        out = zero
        for i, row in enumerate(rows):
            out = jnp.where(sub == i, jnp.sum(row, axis=0, keepdims=True), out)
        return out

    def over_lanes(value):
        for s in (1, 2, 4, 8, 16):
            low = (lane & s) == 0
            value = value + jnp.where(low, pltpu.roll(value, 128 - s, 1), pltpu.roll(value, s, 1))
        return value * inverse_count

    inner = both(sub > 0, sub < ZL - 1)
    early = []
    for i in range(GROUPS):
        u = fields[i][0]

        def whole(y, acc):
            return acc + sum_list([u[x + EDGE, tile(y), :] * u[x + EDGE, tile(y), :] for x in range(NX)])

        def core(y, acc):
            here = [u[x + EDGE, tile(y), :] for x in range(NX)]
            zeroth, next_ = acc
            for x in range(1, NX - 1):
                total = u[x + EDGE, tile(y - 1), :] + u[x + EDGE, tile(y + 1), :]
                total = total + (u[x + EDGE, tile(y, -1), :] + u[x + EDGE, tile(y, 1), :])
                total = total + (here[x - 1] + here[x + 1])
                value = jnp.where(inner, k2[x + EDGE, tile(y), :] * here[x] - total, 0.0)
                mine = jnp.where(inner, here[x], 0.0)
                zeroth, next_ = zeroth + mine * mine, next_ + value * value
            return zeroth, next_
        early.append(lax.fori_loop(0, NY, whole, zero))
        early += list(lax.fori_loop(1, NY - 1, core, (zero, zero)))
    early = jnp.concatenate([stack(early), zero], axis=0)

    pl.semaphore_wait(barrier, greeted)
    send(0, 0)
    send(0, -1)
    send(1, 0)
    phase_start(0, early)
    receive(0, -1)
    kappa_near = ringed(kz[1, 0], [kr[d, 0] for d in range(4)], 1)
    slot(0, 0)
    phase_start(1, phase_end(0))
    slot(1, 0)
    slot(0, 3)

    raw = over_lanes(phase_end(1)[0:8])
    norms, shifts = [], []
    for i in range(GROUPS):
        m0, i0, i1 = (raw[3 * i + j : 3 * i + j + 1] for j in range(3))
        tau = jnp.clip(i1 / jnp.maximum(i0, 1e-30), 0.0, 256.0)
        norms.append(m0)
        shifts.append((tau * m0 / (m0 + EPSILON), tau))

    def refine(i):
        sig, tau = shifts[i]
        e1, e0 = -(sig + tau), sig * tau

        def one(y, acc):
            au, av, akv, aw, akw = acc
            for x in range(NX):
                t = [fields[i][j][x + EDGE, tile(y), :] for j in range(6)]
                v = t[2] - sig * t[0]
                kv_ = t[3] - sig * t[1]
                w = (t[4] + e1 * t[2]) + e0 * t[0]
                kw = (t[5] + e1 * t[3]) + e0 * t[1]
                au, av, akv = au + t[1] * t[1], av + v * v, akv + kv_ * kv_
                aw, akw = aw + w * w, akw + kw * kw
            return au, av, akv, aw, akw
        return lax.fori_loop(0, NY, one, (zero,) * 5)

    low = refine(0)
    slot(1, 3, lambda: phase_start(
        2, jnp.concatenate([stack(low), stack(refine(1))], axis=0)))
    slot(0, 6)
    phase_start(3, phase_end(2))
    slot(1, 6)

    def part(y, _):
        for i in range(GROUPS):
            for x in range(NX):
                t = [fields[i][j][x + EDGE, tile(y), :] for j in range(LAST + 1)]
                for k in range(1, 6):
                    products[i, k - 1, x, pl.ds(y * ZL, ZL), :] = sum_list(
                        [t[j] * t[2 * k - 1 - j] for j in range(k)])
        return 0
    lax.fori_loop(0, NY, part, 0)

    fine = phase_end(3)
    fine = [over_lanes(fine[0:8]), over_lanes(fine[8:16])]
    weights = []
    for i in range(GROUPS):
        cot = []
        for j in range(5):
            row = jnp.zeros((1, 128), jnp.float32)
            for p in range(GP):
                row = jnp.where((lane1 >> 5) == p, cot_ref[j, i * GP + p], row)
            cot.append(row)
        sig, tau = shifts[i]
        e1, e0 = -(sig + tau), sig * tau
        gram = (norms[i],) + tuple(fine[i][j : j + 1] for j in range(5))
        _, back = jax.vjp(lambda *q: scalars(q, (sig, tau, jnp.zeros_like(sig)), cot), *gram)
        _, gpap, gvv, gvav, gww, gwaw = back(jnp.ones((1, 128), jnp.float32))
        sq = e1 * e1 + 2.0 * e0
        weights.append([jnp.broadcast_to(2.0 * c, (ZL, 128)) for c in (
            gpap - 2.0 * sig * gvv + sig * sig * gvav + 2.0 * e1 * e0 * gww + e0 * e0 * gwaw,
            gvv - 2.0 * sig * gvav + sq * gww + 2.0 * e1 * e0 * gwaw,
            gvav + 2.0 * e1 * gww + sq * gwaw,
            gww + 2.0 * e1 * gwaw,
            gwaw,
        )])

    def gather(y, _):
        at = pl.ds(y * ZL, ZL)
        for h in range(2):
            t = [sum_list([weights[i][k] * products[i, k, h * 4 + x, at, :]
                           for i in range(GROUPS) for k in range(5)]) for x in range(4)]
            t = [jnp.where(low2, t[j], t[j + 2])
                 + pltpu.roll(jnp.where(low2, t[j + 2], t[j]), 64, 1) for j in range(2)]
            g[h, at, :] = jnp.where(
                low1, t[0] + pltpu.roll(t[0], 96, 1), t[1] + pltpu.roll(t[1], 32, 1))
        return 0
    lax.fori_loop(0, NY, gather, 0, unroll=True)
    for h in range(2):
        rows = swap_rows_lanes([g[h, y * ZL : y * ZL + ZL, :] for y in range(NY)], lane)
        block = jnp.concatenate(rows, axis=0).T
        for x in range(4):
            for half in range(2):
                at = x * 32 + half * 16
                ov[h * 4 + x, :, half * 128 : half * 128 + 128] = block[at : at + 16, :]
    store = pltpu.make_async_copy(ov, out_ref, lsem.at[2])
    store.start()

    for i, f in [(0, -1)] + [(i, f) for f in range(0, LAST, EDGE) for i in range(GROUPS)]:
        for d in directions(f):
            when(there[d], lambda: copy(i, f, d).wait_send())
    for n in range(4):
        phase_wait(n, lambda c: c.wait_send())
    store.wait()


def body(probes, kappa2, cotangents):
    sizes = tuple(lax.axis_size(a) for a in ("gx", "gy", "gz"))
    f32 = jnp.float32
    any_space = pl.BlockSpec(memory_space=pl.ANY)
    rounds = LAST // EDGE
    return pl.pallas_call(
        functools.partial(kernel, sizes),
        out_shape=jax.ShapeDtypeStruct((NX, NY, NZ), f32),
        in_specs=[any_space, any_space, pl.BlockSpec(memory_space=pltpu.SMEM)],
        out_specs=any_space,
        scratch_shapes=[
            *[pltpu.VMEM((SLABS, ROWS, 128), f32) for _ in range(GROUPS * (LAST + 1))],
            pltpu.VMEM((SLABS, ROWS, 128), f32),
            pltpu.VMEM((2, NY * ZL, 128), f32),
            pltpu.VMEM((GROUPS, 5, NX, NY * ZL, 128), f32),
            pltpu.VMEM((NP, NX, NY, NZ), f32),
            pltpu.VMEM((NX, NY, NZ), f32),
            pltpu.VMEM((2, NY * ZL, 128), f32),
            pltpu.VMEM((NX, NY, NZ), f32),
            pltpu.VMEM((GROUPS, rounds, EDGE, 8, 128), f32),
            pltpu.VMEM((GROUPS, rounds, 4, 2, 8, 128), f32),
            pltpu.VMEM((GROUPS, rounds, 4, 8, 128), f32),
            pltpu.VMEM((GROUPS, rounds, EDGE, 8, 128), f32),
            pltpu.VMEM((NX + 4, TILES + 8, 128), f32),
            pltpu.VMEM((NX + 4, TILES + 8, 128), f32),
            pltpu.VMEM((2, EDGE, 8, 128), f32),
            pltpu.VMEM((4, 2, 8, 128), f32),
            pltpu.VMEM((4, 16, 128), f32),
            pltpu.VMEM((4, 16, 16, 128), f32),
            pltpu.SemaphoreType.DMA((3,)),
            pltpu.SemaphoreType.DMA((GROUPS, rounds, 17)),
            pltpu.SemaphoreType.DMA((GROUPS, rounds, 17)),
            pltpu.SemaphoreType.DMA((2, 13)),
            pltpu.SemaphoreType.DMA((4, 16)),
            pltpu.SemaphoreType.DMA((4, 16)),
        ],
        compiler_params=pltpu.CompilerParams(
            collective_id=0, has_side_effects=True, vmem_limit_bytes=63 << 20
        ),
    )(probes, kappa2, cotangents)


def solution(mesh):
    return jax.shard_map(
        body,
        mesh=mesh,
        in_specs=(P(None, "gx", "gy", "gz"), P("gx", "gy", "gz"), P()),
        out_specs=P("gx", "gy", "gz"),
        check_vma=False,
    )
```

```python
import functools

import jax
import jax.numpy as jnp
from jax import lax
from jax.experimental import pallas as pl
from jax.experimental.pallas import tpu as pltpu
from jax.sharding import PartitionSpec as P

EPSILON = 1e-06
MESH = pl.DeviceIdType.MESH
NP, NX, NY, NZ = 8, 8, 16, 256
GROUPS, GP = 2, 4
ZL, ZH = 8, 32
TOP = 8
EDGE = 3
SLABS, TILES = NX + 2 * EDGE, 24
ROWS = TOP + TILES * ZL + 8
LAST = 9


def scalars(gram, shifts, cot):
    pp, pap, vv, vav, ww, waw = gram
    sig, tau, rho = shifts
    s0 = pp + EPSILON
    a1 = pap / s0
    pv = pap - sig * pp
    d = sig - a1
    b1s = jnp.maximum(vv + 2.0 * d * pv + d * d * pp, 0.0) / s0 + EPSILON
    b1 = jnp.sqrt(b1s)
    scale = s0 * b1s
    pav = vv + sig * pv
    a2 = (vav + 2.0 * d * pav + d * d * pap) / scale - (pv + d * pp) / s0
    b = tau + d - a2
    a = rho + d * sig - b1s - a2 * d
    pw = vv + (sig - tau) * pv - rho * pp
    vw = vav - tau * vv - rho * pv
    b2s = ww + b * b * vv + a * a * pp + 2.0 * (b * vw + a * pw + a * b * pv)
    b2s = jnp.maximum(b2s, 0.0) / scale + EPSILON
    b2 = jnp.sqrt(b2s)
    vaw = ww + tau * vw + rho * pw
    paw = vw + sig * pw
    top = waw + b * b * vav + a * a * pap + 2.0 * (b * vaw + a * paw + a * b * pav)
    cross = vw + b * vv + a * pv + d * (pw + b * pv + a * pp)
    a3 = top / (scale * b2s) - cross / scale
    return cot[0] * a1 + cot[1] * a2 + cot[2] * a3 + cot[3] * b1 + cot[4] * b2


def swap_rows_lanes(arrays, lane):
    arrays = list(arrays)
    for s in (1, 2, 4, 8):
        low = (lane & s) == 0
        for i in range(16):
            if i & s:
                continue
            one, two = arrays[i], arrays[i + s]
            arrays[i] = jnp.where(low, one, pltpu.roll(two, s, 1))
            arrays[i + s] = jnp.where(low, pltpu.roll(one, 128 - s, 1), two)
    return arrays


def sum_list(parts):
    while len(parts) > 1:
        parts = [parts[i] + parts[i + 1] if i + 1 < len(parts) else parts[i]
                 for i in range(0, len(parts), 2)]
    return parts[0]


def kernel(sizes, *refs):
    probes_ref, kappa_ref, cot_ref, out_ref = refs[:4]
    fields = [refs[4 + i * (LAST + 1) : 4 + (i + 1) * (LAST + 1)] for i in range(GROUPS)]
    (k2, g, products, pv, kv, kt, ov, hz, hr, hc, zs, zm, zp, kz, kr, ars, arr,
     lsem, ssem, rsem, ksem, asem, bsem) = refs[4 + GROUPS * (LAST + 1) :]
    nx, ny, nz = sizes
    gx, gy, gz = lax.axis_index("gx"), lax.axis_index("gy"), lax.axis_index("gz")
    inverse_count = 1.0 / (nx * NX * ny * NY * nz * NZ)

    def load(n):
        return pltpu.make_async_copy((probes_ref, kappa_ref)[n], (pv, kv)[n], lsem.at[n])

    load(0).start()
    load(1).start()

    def when(ok, act):
        if ok is None:
            act()
        else:
            pl.when(ok)(act)

    both = jnp.logical_and
    left, right, down, up = gx > 0, gx < nx - 1, gy > 0, gy < ny - 1
    there = (left, right, down, up, None,
             both(left, down), both(left, up), both(right, down), both(right, up),
             left, right, down, up,
             both(left, down), both(left, up), both(right, down), both(right, up),
             both(left, down), both(left, up), both(right, down), both(right, up))
    opposite = (1, 0, 3, 2, 4, 8, 7, 6, 5, 10, 9, 12, 11, 16, 15, 14, 13, 20, 19, 18, 17)
    where_to = (
        lambda: {"gx": gx - 1}, lambda: {"gx": gx + 1}, lambda: {"gy": gy - 1}, lambda: {"gy": gy + 1},
        lambda: {"gz": 1 - gz},
        lambda: {"gx": gx - 1, "gy": gy - 1}, lambda: {"gx": gx - 1, "gy": gy + 1},
        lambda: {"gx": gx + 1, "gy": gy - 1}, lambda: {"gx": gx + 1, "gy": gy + 1},
        lambda: {"gx": gx - 1, "gz": 1 - gz}, lambda: {"gx": gx + 1, "gz": 1 - gz},
        lambda: {"gy": gy - 1, "gz": 1 - gz}, lambda: {"gy": gy + 1, "gz": 1 - gz},
        lambda: {"gx": gx - 1, "gy": gy - 1, "gz": 1 - gz}, lambda: {"gx": gx - 1, "gy": gy + 1, "gz": 1 - gz},
        lambda: {"gx": gx + 1, "gy": gy - 1, "gz": 1 - gz}, lambda: {"gx": gx + 1, "gy": gy + 1, "gz": 1 - gz},
    )
    where_to = where_to + where_to[5:9]

    barrier = pltpu.get_barrier_semaphore()
    group_one = [(i, j) for i in range(nx) for j in range(nz)]

    def greet(where):
        pl.semaphore_signal(barrier, inc=1, device_id=where, device_id_type=MESH)
    greeted = nx * nz - 1 + ny - 1
    for d in (5, 6, 7, 8, 11, 12, 13, 14, 15, 16):
        when(there[d], lambda: greet(where_to[d]()))
        greeted = greeted + there[d].astype(jnp.int32)
    for j in range(ny):
        pl.when(gy != j)(lambda: greet({"gy": j}))
    for i, j in group_one:
        pl.when(jnp.logical_or(gx != i, gz != j))(lambda: greet({"gx": i, "gz": j}))

    lane = lax.broadcasted_iota(jnp.int32, (8, 128), 1)
    sub = lax.broadcasted_iota(jnp.int32, (8, 128), 0)
    lane1 = lax.broadcasted_iota(jnp.int32, (1, 128), 1)
    zero = jnp.zeros((8, 128), jnp.float32)
    first, final = sub == 0, sub == ZL - 1
    zh = lane & (ZH - 1)

    def tile(y, shift=0):
        return pl.ds(TOP + (y + EDGE) * ZL + shift, ZL)

    sent = [u for group in fields for u in group[: LAST : EDGE]]

    def clear(x, y):
        for u in sent:
            u[x + EDGE, tile(y), :] = zero

    def clear_x(x):
        def one(y, _):
            for j in range(EDGE):
                clear(x + j, y)
            return 0
        lax.fori_loop(0, NY, one, 0)

    def clear_y(y):
        def one(x, _):
            for j in range(EDGE):
                clear(x, y + j)
            return 0
        lax.fori_loop(0, NX, one, 0)

    def clear_corner(x, y):
        for j in range(2):
            for k in range(2):
                clear(x + j, y + k)
    pl.when(jnp.logical_not(left))(lambda: clear_x(-EDGE))
    pl.when(jnp.logical_not(right))(lambda: clear_x(NX))
    pl.when(jnp.logical_not(down))(lambda: clear_y(-EDGE))
    pl.when(jnp.logical_not(up))(lambda: clear_y(NY))
    for d, x, y in ((5, -2, -2), (6, -2, NY), (7, NX, -2), (8, NX, NY)):
        pl.when(jnp.logical_not(there[d]))(lambda: clear_corner(x, y))

    load(0).wait()

    def turn_probes(x, _):
        for i in range(GROUPS):
            parts = []
            for p in range(i * GP, (i + 1) * GP):
                parts += [pv[p, x, :, :128], pv[p, x, :, 128:]]
            block = jnp.concatenate(parts, axis=0).T
            rows = swap_rows_lanes([block[j * ZL : j * ZL + ZL, :] for j in range(16)], lane)
            for y in range(NY):
                fields[i][0][x + EDGE, tile(y), :] = rows[y]
        return 0
    lax.fori_loop(0, NX, turn_probes, 0)

    load(1).wait()
    for h in range(2):
        parts = []
        for x in range(h * 4, h * 4 + 4):
            parts += [kv[x, :, :128], kv[x, :, 128:]]
        block = jnp.concatenate(parts, axis=0).T
        rows = swap_rows_lanes([block[j * ZL : j * ZL + ZL, :] for j in range(16)], lane)
        for y in range(NY):
            kt[h, y * ZL : y * ZL + ZL, :] = rows[y] + 6.0

    low2, low1 = (lane & 64) == 0, (lane & 32) == 0

    def spread(y, _):
        for h in range(2):
            row = kt[h, pl.ds(y * ZL, ZL), :]
            turned = pltpu.roll(row, 64, 1)
            for i, two in enumerate((jnp.where(low2, row, turned), jnp.where(low2, turned, row))):
                turned = pltpu.roll(two, 32, 1)
                k2[EDGE + h * 4 + i * 2, tile(y), :] = jnp.where(low1, two, turned)
                k2[EDGE + h * 4 + i * 2 + 1, tile(y), :] = jnp.where(low1, turned, two)
        return 0
    lax.fori_loop(0, NY, spread, 0, unroll=True)

    edge = (ZL - 1) * (1 - gz)
    inward = 2 * gz - 1
    edge_lane = (ZH - 1) * (1 - gz)
    slot_x = ((zh * 11) >> 5) - 1
    slot_y = 8 * (zh - 3 * slot_x - 3) + sub - EDGE
    inside_x, inside_y = both(slot_x >= 0, slot_x < NX), both(slot_y >= 0, slot_y < NY)
    inside = both(inside_x, inside_y)
    beside = (both(slot_x == -1, inside_y), both(slot_x == NX, inside_y),
              both(slot_y == -1, inside_x), both(slot_y == NY, inside_x))
    near = inside
    for d in range(4):
        near = jnp.logical_or(near, both(beside[d], there[d]))

    def packed(u, row):
        out = zero
        for x in range(NX):
            for t in range(2):
                k = 3 * (x + 1) + t
                at = TOP + (EDGE + t * 8) * ZL + row
                moved = pltpu.roll(u[x + EDGE, pl.ds(at, 8, ZL), :], k, 1)
                out = jnp.where(((lane - edge_lane - k) & (ZH - 1)) == 0, moved, out)
        out = jnp.where(gz == 1, out, pltpu.roll(out, 129 - ZH, 1))
        out = pltpu.roll(out, EDGE, 0)
        out = jnp.where(sub < EDGE, pltpu.roll(out, 1, 1), out)
        return jnp.where(inside, out, 0.0)

    def packed_near(u):
        out = zero
        for x in range(-1, NX + 1):
            for t in range(3):
                k = 3 * (x + 1) + t
                row = u[x + EDGE, pl.ds(TOP + t * 8 * ZL + edge, 8, ZL), :]
                moved = pltpu.roll(row, k, 1) if k else row
                out = jnp.where(((lane - edge_lane - k) & (ZH - 1)) == 0, moved, out)
        out = jnp.where(gz == 1, out, pltpu.roll(out, 129 - ZH, 1))
        return jnp.where(near, out, 0.0)

    def copy(i, f, d):
        if f < 0:
            u, width, zsrc, zdst, ring = k2, EDGE - 1, kz.at[0], kz.at[1], kr
            sems = (ksem.at[0, d], ksem.at[1, d])
        else:
            r = f // EDGE
            u, width, zsrc, zdst, ring = fields[i][f], EDGE, zs.at[i, r], hz.at[i, r], hr.at[i, r]
            sems = (ssem.at[i, r, d], rsem.at[i, r, d])
        own_x, own_y = pl.ds(EDGE, NX), pl.ds(TOP + EDGE * ZL, NY * ZL)

        def xs(x):
            return pl.ds(x + EDGE, width)

        def ys(y):
            return pl.ds(TOP + (y + EDGE) * ZL, width * ZL)
        if d == 0:
            src, dst = u.at[xs(0), own_y], u.at[xs(NX), own_y]
        elif d == 1:
            src, dst = u.at[xs(NX - width), own_y], u.at[xs(-width), own_y]
        elif d == 2:
            src, dst = u.at[own_x, ys(0)], u.at[own_x, ys(NY)]
        elif d == 3:
            src, dst = u.at[own_x, ys(NY - width)], u.at[own_x, ys(-width)]
        elif d == 4:
            src, dst = zsrc, zdst
        elif d < 9:
            i_, j_ = (d - 5) // 2, (d - 5) % 2
            src = u.at[(0, NX - 1)[i_] + EDGE, pl.ds(TOP + ((0, NY - 2)[j_] + EDGE) * ZL, 2 * ZL)]
            dst = u.at[(NX, -1)[i_] + EDGE, pl.ds(TOP + ((NY, -2)[j_] + EDGE) * ZL, 2 * ZL)]
        elif d > 16:
            i_, j_ = (d - 17) // 2, (d - 17) % 2
            src = u.at[(1, NX - 2)[i_] + EDGE, tile((0, NY - 1)[j_])]
            dst = u.at[(NX + 1, -2)[i_] + EDGE, tile((NY, -1)[j_])]
        elif d < 13:
            src, dst = zsrc.at[pl.ds(0, 2)], ring.at[opposite[d] - 9]
        else:
            src, dst = zsrc.at[0], hc.at[i, r, opposite[d] - 13]
        return pltpu.make_async_remote_copy(
            src, dst, sems[0], sems[1], device_id=where_to[d](), device_id_type=MESH)

    def directions(f):
        return range(13) if f < 0 else range(21)

    def send(i, f):
        ds = directions(f)
        for d in (*range(5, 9), *range(17, 21), 2, 3):
            if d in ds:
                when(there[d], lambda: copy(i, f, d).start())
        for j in range(EDGE):
            if f < 0:
                kz[0, j] = packed(k2, edge + j * inward)
            else:
                zs[i, f // EDGE, j] = packed(fields[i][f], edge + j * inward)
        for d in (*range(13, 17), *range(9, 13), 4, 0, 1):
            if d in ds:
                when(there[d], lambda: copy(i, f, d).start())

    def receive(i, f):
        for d in directions(f):
            when(there[d], lambda: copy(i, f, opposite[d]).wait_recv())

    edge_low, edge_high = zh == 0, zh == ZH - 1

    def carry_z(u, layer, xs, far=None):
        def aligned(value):
            return jnp.where(gz == 0, pltpu.roll(value, ZH - 1, 1), value)
        layer = aligned(layer)
        if far is not None:
            far = aligned(far)
        under_edge, over_edge = gz == 1, gz == 0
        for x in xs:
            for t in range(3):
                k = 3 * (min(max(x, -1), NX) + 1) + t
                at = TOP + t * 8 * ZL
                halo = layer if -1 <= x <= NX else far
                halo = pltpu.roll(halo, 128 - k, 1) if k else halo
                high = pltpu.roll(u[x + EDGE, pl.ds(at + ZL - 1, 8, ZL), :], 1, 1)
                low = pltpu.roll(u[x + EDGE, pl.ds(at, 8, ZL), :], 127, 1)
                zm[x + 2, t * 8 : t * 8 + 8, :] = jnp.where(
                    edge_low, jnp.where(under_edge, halo, 0.0), high)
                zp[x + 2, t * 8 + 8 : t * 8 + 16, :] = jnp.where(
                    edge_high, jnp.where(over_edge, halo, 0.0), low)

    def main(u, v, ext):
        xs = list(range(-ext, NX + ext))

        def row(y, xs, below, here, above, ok=None):
            done = []
            for x in xs:
                under = jnp.where(first, zm[x + 2, pl.ds(y + EDGE, 8), :], u[x + EDGE, tile(y, -1), :])
                over = jnp.where(final, zp[x + 2, pl.ds(y + EDGE + 1, 8), :], u[x + EDGE, tile(y, 1), :])
                total = (under + over) + (below[x] + above[x]) + (here[x - 1] + here[x + 1])
                value = k2[x + EDGE, tile(y), :] * here[x] - total
                if not 0 <= x < NX:
                    value = jnp.where(left if x < 0 else right, value, 0.0)
                if ok is not None:
                    value = jnp.where(ok, value, 0.0)
                done.append(value)
            for x, value in zip(xs, done):
                v[x + EDGE, tile(y), :] = value

        def read(y, xs):
            return {x: u[x + EDGE, tile(y), :] for x in xs}
        wide = [xs[0] - 1, *xs, xs[-1] + 1]
        for j in range(1, ext + 1):
            for y, ok in ((-j, down), (NY - 1 + j, up)):
                some = list(range(j - ext, NX + ext - j))
                row(y, some, read(y - 1, some), read(y, [some[0] - 1, *some, some[-1] + 1]),
                    read(y + 1, some), ok)

        def pair(q, carry):
            below, here = dict(zip(xs, carry[: len(xs)])), dict(zip(wide, carry[len(xs) :]))
            for y in (2 * q, 2 * q + 1):
                above = read(y + 1, wide)
                row(y, xs, below, here, above)
                below, here = {x: here[x] for x in xs}, above
            return tuple(below[x] for x in xs) + tuple(here[x] for x in wide)
        below, here = read(-1, xs), read(0, wide)
        lax.fori_loop(
            0, NY // 2, pair, tuple(below[x] for x in xs) + tuple(here[x] for x in wide))

    def z_step(here, over, under, kappa, far=None):
        ahead, behind = pltpu.roll(here, 7, 0), pltpu.roll(here, 1, 0)
        ahead = jnp.where(final, pltpu.roll(ahead, 127, 1), ahead)
        behind = jnp.where(first, pltpu.roll(behind, 1, 1), behind)
        lower, higher = pltpu.roll(here, 3, 1), pltpu.roll(here, 125, 1)
        if far is not None:
            lower, higher = jnp.where(slot_x == -1, far, lower), jnp.where(slot_x == NX, far, higher)
        return kappa * here - ((ahead + behind) + (lower + higher) + (over + under))

    def ringed(base, rings, depth):
        for d, turn in ((0, 128 - 3 * NX), (1, 3 * NX), (2, 126), (3, 2)):
            place = beside[d]
            if depth == 2 and d == 2:
                place = both(both(slot_y < 0, slot_y > -3), inside_x)
            elif depth == 2 and d == 3:
                place = both(both(slot_y >= NY, slot_y < NY + 2), inside_x)
            base = jnp.where(both(place, there[d]), pltpu.roll(rings[d], turn, 1), base)
        return base

    def slot(i, f, between=None):
        r = f // EDGE
        u = fields[i][f : f + EDGE + 1]
        receive(i, f)
        layer = ringed(hz[i, r, 0], [hr[i, r, d, 0] for d in range(4)], 2)
        for d, x, y, turn in ((0, -1, -1, -3 * NX - 2), (1, -1, NY, -3 * NX + 2),
                              (2, NX, -1, 3 * NX - 2), (3, NX, NY, 3 * NX + 2)):
            place = both(both(slot_x == x, slot_y == y), there[13 + d])
            layer = jnp.where(place, pltpu.roll(hc[i, r, d], turn % 128, 1), layer)
        far = jnp.where(both(beside[0], left), pltpu.roll(hr[i, r, 0, 0], 128 - 3 * (NX - 1), 1), 0.0)
        far = jnp.where(both(beside[1], right), pltpu.roll(hr[i, r, 1, 0], 3 * (NX - 1), 1), far)
        next_ = ringed(hz[i, r, 1], [hr[i, r, d, 1] for d in range(4)], 1)
        carry_z(u[0], layer, range(-2, NX + 2), far)
        main(u[0], u[1], 2)
        one = jnp.where(near, z_step(layer, next_, packed_near(u[0]), kappa_near, far), 0.0)
        two = jnp.where(inside, z_step(next_, hz[i, r, 2], layer, kz[1, 1]), 0.0)
        carry_z(u[1], one, range(-1, NX + 1))
        main(u[1], u[2], 1)
        if between is not None:
            between()
        one = jnp.where(inside, z_step(one, two, packed(u[1], edge), kz[1, 0]), 0.0)
        carry_z(u[2], one, range(NX))
        main(u[2], u[3], 0)
        if f + EDGE < LAST:
            send(i, f + EDGE)

    def phase_peers(n):
        if n % 2 == 0:
            return [(jnp.logical_or(gx != i, gz != j), i * nz + j, {"gx": i, "gz": j})
                    for i, j in group_one], gx * nz + gz
        return [(gy != j, j, {"gy": j}) for j in range(ny)], gy

    def phase_start(n, value):
        ars[n] = value
        peers, me = phase_peers(n)
        for ok, slot, where in peers:
            pl.when(ok)(lambda: pltpu.make_async_remote_copy(
                ars.at[n], arr.at[n, me], asem.at[n, slot], bsem.at[n, me],
                device_id=where, device_id_type=MESH).start())

    def phase_wait(n, act):
        peers, me = phase_peers(n)
        for ok, slot, where in peers:
            pl.when(ok)(lambda: act(pltpu.make_async_remote_copy(
                ars.at[n], arr.at[n, slot], asem.at[n, slot], bsem.at[n, slot],
                device_id=where, device_id_type=MESH)))
        return peers, me

    def phase_end(n):
        peers, me = phase_wait(n, lambda c: c.wait_recv())
        arr[n, me] = ars[n]
        return sum_list([arr[n, i] for i in range(len(peers))])

    def stack(rows):
        out = zero
        for i, row in enumerate(rows):
            out = jnp.where(sub == i, jnp.sum(row, axis=0, keepdims=True), out)
        return out

    def over_lanes(value):
        for s in (1, 2, 4, 8, 16):
            low = (lane & s) == 0
            value = value + jnp.where(low, pltpu.roll(value, 128 - s, 1), pltpu.roll(value, s, 1))
        return value * inverse_count

    pl.semaphore_wait(barrier, greeted)
    send(0, 0)
    send(0, -1)
    send(1, 0)
    inner = both(sub > 0, sub < ZL - 1)
    early = []
    for i in range(GROUPS):
        u = fields[i][0]

        def whole(y, acc):
            return acc + sum_list([u[x + EDGE, tile(y), :] * u[x + EDGE, tile(y), :] for x in range(NX)])

        def core(y, acc):
            here = [u[x + EDGE, tile(y), :] for x in range(NX)]
            zeroth, next_ = acc
            for x in range(1, NX - 1):
                total = u[x + EDGE, tile(y - 1), :] + u[x + EDGE, tile(y + 1), :]
                total = total + (u[x + EDGE, tile(y, -1), :] + u[x + EDGE, tile(y, 1), :])
                total = total + (here[x - 1] + here[x + 1])
                value = jnp.where(inner, k2[x + EDGE, tile(y), :] * here[x] - total, 0.0)
                mine = jnp.where(inner, here[x], 0.0)
                zeroth, next_ = zeroth + mine * mine, next_ + value * value
            return zeroth, next_
        early.append(lax.fori_loop(0, NY, whole, zero))
        early += list(lax.fori_loop(1, NY - 1, core, (zero, zero)))
    early = jnp.concatenate([stack(early), zero], axis=0)

    phase_start(0, early)
    receive(0, -1)
    kappa_near = ringed(kz[1, 0], [kr[d, 0] for d in range(4)], 1)
    slot(0, 0)
    phase_start(1, phase_end(0))
    slot(1, 0)
    slot(0, 3)

    raw = over_lanes(phase_end(1)[0:8])
    norms, shifts = [], []
    for i in range(GROUPS):
        m0, i0, i1 = (raw[3 * i + j : 3 * i + j + 1] for j in range(3))
        tau = jnp.clip(i1 / jnp.maximum(i0, 1e-30), 0.0, 256.0)
        norms.append(m0)
        shifts.append((tau * m0 / (m0 + EPSILON), tau))

    def refine(i):
        sig, tau = shifts[i]
        e1, e0 = -(sig + tau), sig * tau

        def one(y, acc):
            au, av, akv, aw, akw = acc
            for x in range(NX):
                t = [fields[i][j][x + EDGE, tile(y), :] for j in range(6)]
                v = t[2] - sig * t[0]
                kv_ = t[3] - sig * t[1]
                w = (t[4] + e1 * t[2]) + e0 * t[0]
                kw = (t[5] + e1 * t[3]) + e0 * t[1]
                au, av, akv = au + t[1] * t[1], av + v * v, akv + kv_ * kv_
                aw, akw = aw + w * w, akw + kw * kw
            return au, av, akv, aw, akw
        return lax.fori_loop(0, NY, one, (zero,) * 5)

    low = refine(0)
    slot(1, 3, lambda: phase_start(
        2, jnp.concatenate([stack(low), stack(refine(1))], axis=0)))
    slot(0, 6, lambda: phase_start(3, phase_end(2)))
    slot(1, 6)

    def part(y, _):
        for i in range(GROUPS):
            for x in range(NX):
                t = [fields[i][j][x + EDGE, tile(y), :] for j in range(LAST + 1)]
                for k in range(1, 6):
                    products[i, k - 1, x, pl.ds(y * ZL, ZL), :] = sum_list(
                        [t[j] * t[2 * k - 1 - j] for j in range(k)])
        return 0
    lax.fori_loop(0, NY, part, 0)

    fine = phase_end(3)
    fine = [over_lanes(fine[0:8]), over_lanes(fine[8:16])]
    weights = []
    for i in range(GROUPS):
        cot = []
        for j in range(5):
            row = jnp.zeros((1, 128), jnp.float32)
            for p in range(GP):
                row = jnp.where((lane1 >> 5) == p, cot_ref[j, i * GP + p], row)
            cot.append(row)
        sig, tau = shifts[i]
        e1, e0 = -(sig + tau), sig * tau
        gram = (norms[i],) + tuple(fine[i][j : j + 1] for j in range(5))
        _, back = jax.vjp(lambda *q: scalars(q, (sig, tau, jnp.zeros_like(sig)), cot), *gram)
        _, gpap, gvv, gvav, gww, gwaw = back(jnp.ones((1, 128), jnp.float32))
        sq = e1 * e1 + 2.0 * e0
        weights.append([jnp.broadcast_to(2.0 * c, (ZL, 128)) for c in (
            gpap - 2.0 * sig * gvv + sig * sig * gvav + 2.0 * e1 * e0 * gww + e0 * e0 * gwaw,
            gvv - 2.0 * sig * gvav + sq * gww + 2.0 * e1 * e0 * gwaw,
            gvav + 2.0 * e1 * gww + sq * gwaw,
            gww + 2.0 * e1 * gwaw,
            gwaw,
        )])

    def gather(y, _):
        at = pl.ds(y * ZL, ZL)
        for h in range(2):
            t = [sum_list([weights[i][k] * products[i, k, h * 4 + x, at, :]
                           for i in range(GROUPS) for k in range(5)]) for x in range(4)]
            t = [jnp.where(low2, t[j], t[j + 2])
                 + pltpu.roll(jnp.where(low2, t[j + 2], t[j]), 64, 1) for j in range(2)]
            g[h, at, :] = jnp.where(
                low1, t[0] + pltpu.roll(t[0], 96, 1), t[1] + pltpu.roll(t[1], 32, 1))
        return 0
    lax.fori_loop(0, NY, gather, 0, unroll=True)
    for h in range(2):
        rows = swap_rows_lanes([g[h, y * ZL : y * ZL + ZL, :] for y in range(NY)], lane)
        block = jnp.concatenate(rows, axis=0).T
        for x in range(4):
            for half in range(2):
                at = x * 32 + half * 16
                ov[h * 4 + x, :, half * 128 : half * 128 + 128] = block[at : at + 16, :]
    store = pltpu.make_async_copy(ov, out_ref, lsem.at[2])
    store.start()

    for i, f in [(0, -1)] + [(i, f) for f in range(0, LAST, EDGE) for i in range(GROUPS)]:
        for d in directions(f):
            when(there[d], lambda: copy(i, f, d).wait_send())
    for n in range(4):
        phase_wait(n, lambda c: c.wait_send())
    store.wait()


def body(probes, kappa2, cotangents):
    sizes = tuple(lax.axis_size(a) for a in ("gx", "gy", "gz"))
    f32 = jnp.float32
    any_space = pl.BlockSpec(memory_space=pl.ANY)
    rounds = LAST // EDGE
    return pl.pallas_call(
        functools.partial(kernel, sizes),
        out_shape=jax.ShapeDtypeStruct((NX, NY, NZ), f32),
        in_specs=[any_space, any_space, pl.BlockSpec(memory_space=pltpu.SMEM)],
        out_specs=any_space,
        scratch_shapes=[
            *[pltpu.VMEM((SLABS, ROWS, 128), f32) for _ in range(GROUPS * (LAST + 1))],
            pltpu.VMEM((SLABS, ROWS, 128), f32),
            pltpu.VMEM((2, NY * ZL, 128), f32),
            pltpu.VMEM((GROUPS, 5, NX, NY * ZL, 128), f32),
            pltpu.VMEM((NP, NX, NY, NZ), f32),
            pltpu.VMEM((NX, NY, NZ), f32),
            pltpu.VMEM((2, NY * ZL, 128), f32),
            pltpu.VMEM((NX, NY, NZ), f32),
            pltpu.VMEM((GROUPS, rounds, EDGE, 8, 128), f32),
            pltpu.VMEM((GROUPS, rounds, 4, 2, 8, 128), f32),
            pltpu.VMEM((GROUPS, rounds, 4, 8, 128), f32),
            pltpu.VMEM((GROUPS, rounds, EDGE, 8, 128), f32),
            pltpu.VMEM((NX + 4, TILES + 8, 128), f32),
            pltpu.VMEM((NX + 4, TILES + 8, 128), f32),
            pltpu.VMEM((2, EDGE, 8, 128), f32),
            pltpu.VMEM((4, 2, 8, 128), f32),
            pltpu.VMEM((4, 16, 128), f32),
            pltpu.VMEM((4, 16, 16, 128), f32),
            pltpu.SemaphoreType.DMA((3,)),
            pltpu.SemaphoreType.DMA((GROUPS, rounds, 21)),
            pltpu.SemaphoreType.DMA((GROUPS, rounds, 21)),
            pltpu.SemaphoreType.DMA((2, 13)),
            pltpu.SemaphoreType.DMA((4, 16)),
            pltpu.SemaphoreType.DMA((4, 16)),
        ],
        compiler_params=pltpu.CompilerParams(
            collective_id=0, has_side_effects=True, vmem_limit_bytes=63 << 20
        ),
    )(probes, kappa2, cotangents)


def solution(mesh):
    return jax.shard_map(
        body,
        mesh=mesh,
        in_specs=(P(None, "gx", "gy", "gz"), P("gx", "gy", "gz"), P()),
        out_specs=P("gx", "gy", "gz"),
        check_vma=False,
    )
```

```python
import functools

import jax
import jax.numpy as jnp
from jax import lax
from jax.experimental import pallas as pl
from jax.experimental.pallas import tpu as pltpu
from jax.sharding import PartitionSpec as P

EPSILON = 1e-06
MESH = pl.DeviceIdType.MESH
NP, NX, NY, NZ = 8, 8, 16, 256
GROUPS, GP = 2, 4
ZL, ZH = 8, 32
TOP = 8
EDGE = 3
SLABS, TILES = NX + 2 * EDGE, 24
ROWS = TOP + TILES * ZL + 8
LAST = 9


def scalars(gram, shifts, cot):
    pp, pap, vv, vav, ww, waw = gram
    sig, tau, rho = shifts
    s0 = pp + EPSILON
    a1 = pap / s0
    pv = pap - sig * pp
    d = sig - a1
    b1s = jnp.maximum(vv + 2.0 * d * pv + d * d * pp, 0.0) / s0 + EPSILON
    b1 = jnp.sqrt(b1s)
    scale = s0 * b1s
    pav = vv + sig * pv
    a2 = (vav + 2.0 * d * pav + d * d * pap) / scale - (pv + d * pp) / s0
    b = tau + d - a2
    a = rho + d * sig - b1s - a2 * d
    pw = vv + (sig - tau) * pv - rho * pp
    vw = vav - tau * vv - rho * pv
    b2s = ww + b * b * vv + a * a * pp + 2.0 * (b * vw + a * pw + a * b * pv)
    b2s = jnp.maximum(b2s, 0.0) / scale + EPSILON
    b2 = jnp.sqrt(b2s)
    vaw = ww + tau * vw + rho * pw
    paw = vw + sig * pw
    top = waw + b * b * vav + a * a * pap + 2.0 * (b * vaw + a * paw + a * b * pav)
    cross = vw + b * vv + a * pv + d * (pw + b * pv + a * pp)
    a3 = top / (scale * b2s) - cross / scale
    return cot[0] * a1 + cot[1] * a2 + cot[2] * a3 + cot[3] * b1 + cot[4] * b2


def swap_rows_lanes(arrays, lane):
    arrays = list(arrays)
    for s in (1, 2, 4, 8):
        low = (lane & s) == 0
        for i in range(16):
            if i & s:
                continue
            one, two = arrays[i], arrays[i + s]
            arrays[i] = jnp.where(low, one, pltpu.roll(two, s, 1))
            arrays[i + s] = jnp.where(low, pltpu.roll(one, 128 - s, 1), two)
    return arrays


def sum_list(parts):
    while len(parts) > 1:
        parts = [parts[i] + parts[i + 1] if i + 1 < len(parts) else parts[i]
                 for i in range(0, len(parts), 2)]
    return parts[0]


def kernel(sizes, *refs):
    probes_ref, kappa_ref, cot_ref, out_ref = refs[:4]
    fields = [refs[4 + i * (LAST + 1) : 4 + (i + 1) * (LAST + 1)] for i in range(GROUPS)]
    (k2, g, products, pv, kv, kt, ov, hz, hr, hc, zs, zm, zp, kz, kr, ars, arr,
     lsem, ssem, rsem, ksem, asem, bsem) = refs[4 + GROUPS * (LAST + 1) :]
    nx, ny, nz = sizes
    gx, gy, gz = lax.axis_index("gx"), lax.axis_index("gy"), lax.axis_index("gz")
    inverse_count = 1.0 / (nx * NX * ny * NY * nz * NZ)

    def load(n):
        return pltpu.make_async_copy((probes_ref, kappa_ref)[n], (pv, kv)[n], lsem.at[n])

    load(0).start()
    load(1).start()

    def when(ok, act):
        if ok is None:
            act()
        else:
            pl.when(ok)(act)

    both = jnp.logical_and
    left, right, down, up = gx > 0, gx < nx - 1, gy > 0, gy < ny - 1
    there = (left, right, down, up, None,
             both(left, down), both(left, up), both(right, down), both(right, up),
             left, right, down, up,
             both(left, down), both(left, up), both(right, down), both(right, up),
             both(left, down), both(left, up), both(right, down), both(right, up))
    opposite = (1, 0, 3, 2, 4, 8, 7, 6, 5, 10, 9, 12, 11, 16, 15, 14, 13, 20, 19, 18, 17)
    where_to = (
        lambda: {"gx": gx - 1}, lambda: {"gx": gx + 1}, lambda: {"gy": gy - 1}, lambda: {"gy": gy + 1},
        lambda: {"gz": 1 - gz},
        lambda: {"gx": gx - 1, "gy": gy - 1}, lambda: {"gx": gx - 1, "gy": gy + 1},
        lambda: {"gx": gx + 1, "gy": gy - 1}, lambda: {"gx": gx + 1, "gy": gy + 1},
        lambda: {"gx": gx - 1, "gz": 1 - gz}, lambda: {"gx": gx + 1, "gz": 1 - gz},
        lambda: {"gy": gy - 1, "gz": 1 - gz}, lambda: {"gy": gy + 1, "gz": 1 - gz},
        lambda: {"gx": gx - 1, "gy": gy - 1, "gz": 1 - gz}, lambda: {"gx": gx - 1, "gy": gy + 1, "gz": 1 - gz},
        lambda: {"gx": gx + 1, "gy": gy - 1, "gz": 1 - gz}, lambda: {"gx": gx + 1, "gy": gy + 1, "gz": 1 - gz},
    )
    where_to = where_to + where_to[5:9]

    barrier = pltpu.get_barrier_semaphore()
    group_one = [(i, j) for i in range(nx) for j in range(nz)]

    def greet(where):
        pl.semaphore_signal(barrier, inc=1, device_id=where, device_id_type=MESH)
    greeted = nx * nz - 1 + ny - 1
    for d in (5, 6, 7, 8, 11, 12, 13, 14, 15, 16):
        when(there[d], lambda: greet(where_to[d]()))
        greeted = greeted + there[d].astype(jnp.int32)
    for j in range(ny):
        pl.when(gy != j)(lambda: greet({"gy": j}))
    for i, j in group_one:
        pl.when(jnp.logical_or(gx != i, gz != j))(lambda: greet({"gx": i, "gz": j}))

    lane = lax.broadcasted_iota(jnp.int32, (8, 128), 1)
    sub = lax.broadcasted_iota(jnp.int32, (8, 128), 0)
    lane1 = lax.broadcasted_iota(jnp.int32, (1, 128), 1)
    zero = jnp.zeros((8, 128), jnp.float32)
    first, final = sub == 0, sub == ZL - 1
    zh = lane & (ZH - 1)

    def tile(y, shift=0):
        return pl.ds(TOP + (y + EDGE) * ZL + shift, ZL)

    sent = [u for group in fields for u in group[: LAST : EDGE]]

    def clear(x, y):
        for u in sent:
            u[x + EDGE, tile(y), :] = zero

    def clear_x(x):
        def one(y, _):
            for j in range(EDGE):
                clear(x + j, y)
            return 0
        lax.fori_loop(0, NY, one, 0)

    def clear_y(y):
        def one(x, _):
            for j in range(EDGE):
                clear(x, y + j)
            return 0
        lax.fori_loop(0, NX, one, 0)

    def clear_corner(x, y):
        for j in range(2):
            for k in range(2):
                clear(x + j, y + k)
    pl.when(jnp.logical_not(left))(lambda: clear_x(-EDGE))
    pl.when(jnp.logical_not(right))(lambda: clear_x(NX))
    pl.when(jnp.logical_not(down))(lambda: clear_y(-EDGE))
    pl.when(jnp.logical_not(up))(lambda: clear_y(NY))
    for d, x, y in ((5, -2, -2), (6, -2, NY), (7, NX, -2), (8, NX, NY)):
        pl.when(jnp.logical_not(there[d]))(lambda: clear_corner(x, y))

    load(0).wait()

    def turn_probes(x, _):
        for i in range(GROUPS):
            parts = []
            for p in range(i * GP, (i + 1) * GP):
                parts += [pv[p, x, :, :128], pv[p, x, :, 128:]]
            block = jnp.concatenate(parts, axis=0).T
            rows = swap_rows_lanes([block[j * ZL : j * ZL + ZL, :] for j in range(16)], lane)
            for y in range(NY):
                fields[i][0][x + EDGE, tile(y), :] = rows[y]
        return 0
    lax.fori_loop(0, NX, turn_probes, 0)

    load(1).wait()
    for h in range(2):
        parts = []
        for x in range(h * 4, h * 4 + 4):
            parts += [kv[x, :, :128], kv[x, :, 128:]]
        block = jnp.concatenate(parts, axis=0).T
        rows = swap_rows_lanes([block[j * ZL : j * ZL + ZL, :] for j in range(16)], lane)
        for y in range(NY):
            kt[h, y * ZL : y * ZL + ZL, :] = rows[y] + 6.0

    low2, low1 = (lane & 64) == 0, (lane & 32) == 0

    def spread(y, _):
        for h in range(2):
            row = kt[h, pl.ds(y * ZL, ZL), :]
            turned = pltpu.roll(row, 64, 1)
            for i, two in enumerate((jnp.where(low2, row, turned), jnp.where(low2, turned, row))):
                turned = pltpu.roll(two, 32, 1)
                k2[EDGE + h * 4 + i * 2, tile(y), :] = jnp.where(low1, two, turned)
                k2[EDGE + h * 4 + i * 2 + 1, tile(y), :] = jnp.where(low1, turned, two)
        return 0
    lax.fori_loop(0, NY, spread, 0, unroll=True)

    edge = (ZL - 1) * (1 - gz)
    inward = 2 * gz - 1
    edge_lane = (ZH - 1) * (1 - gz)
    slot_x = ((zh * 11) >> 5) - 1
    slot_y = 8 * (zh - 3 * slot_x - 3) + sub - EDGE
    inside_x, inside_y = both(slot_x >= 0, slot_x < NX), both(slot_y >= 0, slot_y < NY)
    inside = both(inside_x, inside_y)
    beside = (both(slot_x == -1, inside_y), both(slot_x == NX, inside_y),
              both(slot_y == -1, inside_x), both(slot_y == NY, inside_x))
    near = inside
    for d in range(4):
        near = jnp.logical_or(near, both(beside[d], there[d]))

    def packed(u, row):
        out = zero
        for x in range(NX):
            for t in range(2):
                k = 3 * (x + 1) + t
                at = TOP + (EDGE + t * 8) * ZL + row
                moved = pltpu.roll(u[x + EDGE, pl.ds(at, 8, ZL), :], k, 1)
                out = jnp.where(((lane - edge_lane - k) & (ZH - 1)) == 0, moved, out)
        out = jnp.where(gz == 1, out, pltpu.roll(out, 129 - ZH, 1))
        out = pltpu.roll(out, EDGE, 0)
        out = jnp.where(sub < EDGE, pltpu.roll(out, 1, 1), out)
        return jnp.where(inside, out, 0.0)

    def packed_near(u):
        out = zero
        for x in range(-1, NX + 1):
            for t in range(3):
                k = 3 * (x + 1) + t
                row = u[x + EDGE, pl.ds(TOP + t * 8 * ZL + edge, 8, ZL), :]
                moved = pltpu.roll(row, k, 1) if k else row
                out = jnp.where(((lane - edge_lane - k) & (ZH - 1)) == 0, moved, out)
        out = jnp.where(gz == 1, out, pltpu.roll(out, 129 - ZH, 1))
        return jnp.where(near, out, 0.0)

    def copy(i, f, d):
        if f < 0:
            u, width, zsrc, zdst, ring = k2, EDGE - 1, kz.at[0, pl.ds(0, 2)], kz.at[1, pl.ds(0, 2)], kr
            sems = (ksem.at[0, d], ksem.at[1, d])
        else:
            r = f // EDGE
            u, width, zsrc, zdst, ring = fields[i][f], EDGE, zs.at[i, r], hz.at[i, r], hr.at[i, r]
            sems = (ssem.at[i, r, d], rsem.at[i, r, d])
        own_x, own_y = pl.ds(EDGE, NX), pl.ds(TOP + EDGE * ZL, NY * ZL)

        def xs(x):
            return pl.ds(x + EDGE, width)

        def ys(y):
            return pl.ds(TOP + (y + EDGE) * ZL, width * ZL)
        if d == 0:
            src, dst = u.at[xs(0), own_y], u.at[xs(NX), own_y]
        elif d == 1:
            src, dst = u.at[xs(NX - width), own_y], u.at[xs(-width), own_y]
        elif d == 2:
            src, dst = u.at[own_x, ys(0)], u.at[own_x, ys(NY)]
        elif d == 3:
            src, dst = u.at[own_x, ys(NY - width)], u.at[own_x, ys(-width)]
        elif d == 4:
            src, dst = zsrc, zdst
        elif d < 9:
            i_, j_ = (d - 5) // 2, (d - 5) % 2
            src = u.at[(0, NX - 1)[i_] + EDGE, pl.ds(TOP + ((0, NY - 2)[j_] + EDGE) * ZL, 2 * ZL)]
            dst = u.at[(NX, -1)[i_] + EDGE, pl.ds(TOP + ((NY, -2)[j_] + EDGE) * ZL, 2 * ZL)]
        elif d > 16:
            i_, j_ = (d - 17) // 2, (d - 17) % 2
            src = u.at[(1, NX - 2)[i_] + EDGE, tile((0, NY - 1)[j_])]
            dst = u.at[(NX + 1, -2)[i_] + EDGE, tile((NY, -1)[j_])]
        elif d < 13:
            src, dst = zsrc.at[pl.ds(0, 2)], ring.at[opposite[d] - 9]
        else:
            src, dst = zsrc.at[0], hc.at[i, r, opposite[d] - 13]
        return pltpu.make_async_remote_copy(
            src, dst, sems[0], sems[1], device_id=where_to[d](), device_id_type=MESH)

    def directions(f):
        return range(13) if f < 0 else range(21)

    def send(i, f):
        ds = directions(f)
        for d in (*range(5, 9), *range(17, 21), 2, 3, *((0, 1) if f < 0 else ())):
            if d in ds:
                when(there[d], lambda: copy(i, f, d).start())
        for j in range(2 if f < 0 else EDGE):
            if f < 0:
                kz[0, j] = packed(k2, edge + j * inward)
            else:
                zs[i, f // EDGE, j] = packed(fields[i][f], edge + j * inward)
        for d in (*range(13, 17), *range(9, 13), 4, *(() if f < 0 else (0, 1))):
            if d in ds:
                when(there[d], lambda: copy(i, f, d).start())

    def receive(i, f):
        for d in directions(f):
            when(there[d], lambda: copy(i, f, opposite[d]).wait_recv())

    edge_low, edge_high = zh == 0, zh == ZH - 1

    def carry_z(u, layer, xs, far=None):
        def aligned(value):
            return jnp.where(gz == 0, pltpu.roll(value, ZH - 1, 1), value)
        layer = aligned(layer)
        if far is not None:
            far = aligned(far)
        under_edge, over_edge = gz == 1, gz == 0
        for x in xs:
            for t in range(3):
                k = 3 * (min(max(x, -1), NX) + 1) + t
                at = TOP + t * 8 * ZL
                halo = layer if -1 <= x <= NX else far
                halo = pltpu.roll(halo, 128 - k, 1) if k else halo
                high = pltpu.roll(u[x + EDGE, pl.ds(at + ZL - 1, 8, ZL), :], 1, 1)
                low = pltpu.roll(u[x + EDGE, pl.ds(at, 8, ZL), :], 127, 1)
                zm[x + 2, t * 8 : t * 8 + 8, :] = jnp.where(
                    edge_low, jnp.where(under_edge, halo, 0.0), high)
                zp[x + 2, t * 8 + 8 : t * 8 + 16, :] = jnp.where(
                    edge_high, jnp.where(over_edge, halo, 0.0), low)

    def main(u, v, ext):
        xs = list(range(-ext, NX + ext))

        def row(y, xs, below, here, above, ok=None):
            done = []
            for x in xs:
                under = jnp.where(first, zm[x + 2, pl.ds(y + EDGE, 8), :], u[x + EDGE, tile(y, -1), :])
                over = jnp.where(final, zp[x + 2, pl.ds(y + EDGE + 1, 8), :], u[x + EDGE, tile(y, 1), :])
                total = (under + over) + (below[x] + above[x]) + (here[x - 1] + here[x + 1])
                value = k2[x + EDGE, tile(y), :] * here[x] - total
                if not 0 <= x < NX:
                    value = jnp.where(left if x < 0 else right, value, 0.0)
                if ok is not None:
                    value = jnp.where(ok, value, 0.0)
                done.append(value)
            for x, value in zip(xs, done):
                v[x + EDGE, tile(y), :] = value

        def read(y, xs):
            return {x: u[x + EDGE, tile(y), :] for x in xs}
        wide = [xs[0] - 1, *xs, xs[-1] + 1]
        for j in range(1, ext + 1):
            for y, ok in ((-j, down), (NY - 1 + j, up)):
                some = list(range(j - ext, NX + ext - j))
                row(y, some, read(y - 1, some), read(y, [some[0] - 1, *some, some[-1] + 1]),
                    read(y + 1, some), ok)

        def pair(q, carry):
            below, here = dict(zip(xs, carry[: len(xs)])), dict(zip(wide, carry[len(xs) :]))
            for y in (2 * q, 2 * q + 1):
                above = read(y + 1, wide)
                row(y, xs, below, here, above)
                below, here = {x: here[x] for x in xs}, above
            return tuple(below[x] for x in xs) + tuple(here[x] for x in wide)
        below, here = read(-1, xs), read(0, wide)
        lax.fori_loop(
            0, NY // 2, pair, tuple(below[x] for x in xs) + tuple(here[x] for x in wide))

    def z_step(here, over, under, kappa, far=None):
        ahead, behind = pltpu.roll(here, 7, 0), pltpu.roll(here, 1, 0)
        ahead = jnp.where(final, pltpu.roll(ahead, 127, 1), ahead)
        behind = jnp.where(first, pltpu.roll(behind, 1, 1), behind)
        lower, higher = pltpu.roll(here, 3, 1), pltpu.roll(here, 125, 1)
        if far is not None:
            lower, higher = jnp.where(slot_x == -1, far, lower), jnp.where(slot_x == NX, far, higher)
        return kappa * here - ((ahead + behind) + (lower + higher) + (over + under))

    def ringed(base, rings, depth):
        for d, turn in ((0, 128 - 3 * NX), (1, 3 * NX), (2, 126), (3, 2)):
            place = beside[d]
            if depth == 2 and d == 2:
                place = both(both(slot_y < 0, slot_y > -3), inside_x)
            elif depth == 2 and d == 3:
                place = both(both(slot_y >= NY, slot_y < NY + 2), inside_x)
            base = jnp.where(both(place, there[d]), pltpu.roll(rings[d], turn, 1), base)
        return base

    def slot(i, f, between=None):
        r = f // EDGE
        u = fields[i][f : f + EDGE + 1]
        receive(i, f)
        layer = ringed(hz[i, r, 0], [hr[i, r, d, 0] for d in range(4)], 2)
        for d, x, y, turn in ((0, -1, -1, -3 * NX - 2), (1, -1, NY, -3 * NX + 2),
                              (2, NX, -1, 3 * NX - 2), (3, NX, NY, 3 * NX + 2)):
            place = both(both(slot_x == x, slot_y == y), there[13 + d])
            layer = jnp.where(place, pltpu.roll(hc[i, r, d], turn % 128, 1), layer)
        far = jnp.where(both(beside[0], left), pltpu.roll(hr[i, r, 0, 0], 128 - 3 * (NX - 1), 1), 0.0)
        far = jnp.where(both(beside[1], right), pltpu.roll(hr[i, r, 1, 0], 3 * (NX - 1), 1), far)
        next_ = ringed(hz[i, r, 1], [hr[i, r, d, 1] for d in range(4)], 1)
        carry_z(u[0], layer, range(-2, NX + 2), far)
        main(u[0], u[1], 2)
        one = jnp.where(near, z_step(layer, next_, packed_near(u[0]), kappa_near, far), 0.0)
        two = jnp.where(inside, z_step(next_, hz[i, r, 2], layer, kz[1, 1]), 0.0)
        carry_z(u[1], one, range(-1, NX + 1))
        main(u[1], u[2], 1)
        if between is not None:
            between()
        one = jnp.where(inside, z_step(one, two, packed(u[1], edge), kz[1, 0]), 0.0)
        carry_z(u[2], one, range(NX))
        main(u[2], u[3], 0)
        if f + EDGE < LAST:
            send(i, f + EDGE)

    def phase_peers(n):
        if n % 2 == 0:
            return [(jnp.logical_or(gx != i, gz != j), i * nz + j, {"gx": i, "gz": j})
                    for i, j in group_one], gx * nz + gz
        return [(gy != j, j, {"gy": j}) for j in range(ny)], gy

    def phase_start(n, value):
        ars[n] = value
        peers, me = phase_peers(n)
        for ok, slot, where in peers:
            pl.when(ok)(lambda: pltpu.make_async_remote_copy(
                ars.at[n], arr.at[n, me], asem.at[n, slot], bsem.at[n, me],
                device_id=where, device_id_type=MESH).start())

    def phase_wait(n, act):
        peers, me = phase_peers(n)
        for ok, slot, where in peers:
            pl.when(ok)(lambda: act(pltpu.make_async_remote_copy(
                ars.at[n], arr.at[n, slot], asem.at[n, slot], bsem.at[n, slot],
                device_id=where, device_id_type=MESH)))
        return peers, me

    def phase_end(n):
        peers, me = phase_wait(n, lambda c: c.wait_recv())
        arr[n, me] = ars[n]
        return sum_list([arr[n, i] for i in range(len(peers))])

    def stack(rows):
        out = zero
        for i, row in enumerate(rows):
            out = jnp.where(sub == i, jnp.sum(row, axis=0, keepdims=True), out)
        return out

    def over_lanes(value):
        for s in (1, 2, 4, 8, 16):
            low = (lane & s) == 0
            value = value + jnp.where(low, pltpu.roll(value, 128 - s, 1), pltpu.roll(value, s, 1))
        return value * inverse_count

    pl.semaphore_wait(barrier, greeted)
    send(0, 0)
    send(0, -1)
    send(1, 0)
    inner = both(sub > 0, sub < ZL - 1)
    early = []
    for i in range(GROUPS):
        u = fields[i][0]

        def whole(y, acc):
            return acc + sum_list([u[x + EDGE, tile(y), :] * u[x + EDGE, tile(y), :] for x in range(NX)])

        def core(y, acc):
            here = [u[x + EDGE, tile(y), :] for x in range(NX)]
            zeroth, next_ = acc
            for x in range(1, NX - 1):
                total = u[x + EDGE, tile(y - 1), :] + u[x + EDGE, tile(y + 1), :]
                total = total + (u[x + EDGE, tile(y, -1), :] + u[x + EDGE, tile(y, 1), :])
                total = total + (here[x - 1] + here[x + 1])
                value = jnp.where(inner, k2[x + EDGE, tile(y), :] * here[x] - total, 0.0)
                mine = jnp.where(inner, here[x], 0.0)
                zeroth, next_ = zeroth + mine * mine, next_ + value * value
            return zeroth, next_
        early.append(lax.fori_loop(0, NY, whole, zero))
        early += list(lax.fori_loop(1, NY - 1, core, (zero, zero)))
    early = jnp.concatenate([stack(early), zero], axis=0)

    phase_start(0, early)
    receive(0, -1)
    kappa_near = ringed(kz[1, 0], [kr[d, 0] for d in range(4)], 1)
    slot(0, 0)
    phase_start(1, phase_end(0))
    slot(1, 0)
    slot(0, 3)

    raw = over_lanes(phase_end(1)[0:8])
    norms, shifts = [], []
    for i in range(GROUPS):
        m0, i0, i1 = (raw[3 * i + j : 3 * i + j + 1] for j in range(3))
        tau = jnp.clip(i1 / jnp.maximum(i0, 1e-30), 0.0, 256.0)
        norms.append(m0)
        shifts.append((tau * m0 / (m0 + EPSILON), tau))

    def refine(i):
        sig, tau = shifts[i]
        e1, e0 = -(sig + tau), sig * tau

        def one(y, acc):
            au, av, akv, aw, akw = acc
            for x in range(NX):
                t = [fields[i][j][x + EDGE, tile(y), :] for j in range(6)]
                v = t[2] - sig * t[0]
                kv_ = t[3] - sig * t[1]
                w = (t[4] + e1 * t[2]) + e0 * t[0]
                kw = (t[5] + e1 * t[3]) + e0 * t[1]
                au, av, akv = au + t[1] * t[1], av + v * v, akv + kv_ * kv_
                aw, akw = aw + w * w, akw + kw * kw
            return au, av, akv, aw, akw
        return lax.fori_loop(0, NY, one, (zero,) * 5)

    low = refine(0)
    slot(1, 3, lambda: phase_start(
        2, jnp.concatenate([stack(low), stack(refine(1))], axis=0)))
    slot(0, 6, lambda: phase_start(3, phase_end(2)))
    slot(1, 6)

    def part(y, _):
        for i in range(GROUPS):
            for x in range(NX):
                t = [fields[i][j][x + EDGE, tile(y), :] for j in range(LAST + 1)]
                for k in range(1, 6):
                    products[i, k - 1, x, pl.ds(y * ZL, ZL), :] = sum_list(
                        [t[j] * t[2 * k - 1 - j] for j in range(k)])
        return 0
    lax.fori_loop(0, NY, part, 0)

    fine = phase_end(3)
    fine = [over_lanes(fine[0:8]), over_lanes(fine[8:16])]
    weights = []
    for i in range(GROUPS):
        cot = []
        for j in range(5):
            row = jnp.zeros((1, 128), jnp.float32)
            for p in range(GP):
                row = jnp.where((lane1 >> 5) == p, cot_ref[j, i * GP + p], row)
            cot.append(row)
        sig, tau = shifts[i]
        e1, e0 = -(sig + tau), sig * tau
        gram = (norms[i],) + tuple(fine[i][j : j + 1] for j in range(5))
        _, back = jax.vjp(lambda *q: scalars(q, (sig, tau, jnp.zeros_like(sig)), cot), *gram)
        _, gpap, gvv, gvav, gww, gwaw = back(jnp.ones((1, 128), jnp.float32))
        sq = e1 * e1 + 2.0 * e0
        weights.append([jnp.broadcast_to(2.0 * c, (ZL, 128)) for c in (
            gpap - 2.0 * sig * gvv + sig * sig * gvav + 2.0 * e1 * e0 * gww + e0 * e0 * gwaw,
            gvv - 2.0 * sig * gvav + sq * gww + 2.0 * e1 * e0 * gwaw,
            gvav + 2.0 * e1 * gww + sq * gwaw,
            gww + 2.0 * e1 * gwaw,
            gwaw,
        )])

    def gather(y, _):
        at = pl.ds(y * ZL, ZL)
        for h in range(2):
            t = [sum_list([weights[i][k] * products[i, k, h * 4 + x, at, :]
                           for i in range(GROUPS) for k in range(5)]) for x in range(4)]
            t = [jnp.where(low2, t[j], t[j + 2])
                 + pltpu.roll(jnp.where(low2, t[j + 2], t[j]), 64, 1) for j in range(2)]
            g[h, at, :] = jnp.where(
                low1, t[0] + pltpu.roll(t[0], 96, 1), t[1] + pltpu.roll(t[1], 32, 1))
        return 0
    lax.fori_loop(0, NY, gather, 0, unroll=True)
    for h in range(2):
        rows = swap_rows_lanes([g[h, y * ZL : y * ZL + ZL, :] for y in range(NY)], lane)
        block = jnp.concatenate(rows, axis=0).T
        for x in range(4):
            for half in range(2):
                at = x * 32 + half * 16
                ov[h * 4 + x, :, half * 128 : half * 128 + 128] = block[at : at + 16, :]
    store = pltpu.make_async_copy(ov, out_ref, lsem.at[2])
    store.start()

    for i, f in [(0, -1)] + [(i, f) for f in range(0, LAST, EDGE) for i in range(GROUPS)]:
        for d in directions(f):
            when(there[d], lambda: copy(i, f, d).wait_send())
    for n in range(4):
        phase_wait(n, lambda c: c.wait_send())
    store.wait()


def body(probes, kappa2, cotangents):
    sizes = tuple(lax.axis_size(a) for a in ("gx", "gy", "gz"))
    f32 = jnp.float32
    any_space = pl.BlockSpec(memory_space=pl.ANY)
    rounds = LAST // EDGE
    return pl.pallas_call(
        functools.partial(kernel, sizes),
        out_shape=jax.ShapeDtypeStruct((NX, NY, NZ), f32),
        in_specs=[any_space, any_space, pl.BlockSpec(memory_space=pltpu.SMEM)],
        out_specs=any_space,
        scratch_shapes=[
            *[pltpu.VMEM((SLABS, ROWS, 128), f32) for _ in range(GROUPS * (LAST + 1))],
            pltpu.VMEM((SLABS, ROWS, 128), f32),
            pltpu.VMEM((2, NY * ZL, 128), f32),
            pltpu.VMEM((GROUPS, 5, NX, NY * ZL, 128), f32),
            pltpu.VMEM((NP, NX, NY, NZ), f32),
            pltpu.VMEM((NX, NY, NZ), f32),
            pltpu.VMEM((2, NY * ZL, 128), f32),
            pltpu.VMEM((NX, NY, NZ), f32),
            pltpu.VMEM((GROUPS, rounds, EDGE, 8, 128), f32),
            pltpu.VMEM((GROUPS, rounds, 4, 2, 8, 128), f32),
            pltpu.VMEM((GROUPS, rounds, 4, 8, 128), f32),
            pltpu.VMEM((GROUPS, rounds, EDGE, 8, 128), f32),
            pltpu.VMEM((NX + 4, TILES + 8, 128), f32),
            pltpu.VMEM((NX + 4, TILES + 8, 128), f32),
            pltpu.VMEM((2, EDGE, 8, 128), f32),
            pltpu.VMEM((4, 2, 8, 128), f32),
            pltpu.VMEM((4, 16, 128), f32),
            pltpu.VMEM((4, 16, 16, 128), f32),
            pltpu.SemaphoreType.DMA((3,)),
            pltpu.SemaphoreType.DMA((GROUPS, rounds, 21)),
            pltpu.SemaphoreType.DMA((GROUPS, rounds, 21)),
            pltpu.SemaphoreType.DMA((2, 13)),
            pltpu.SemaphoreType.DMA((4, 16)),
            pltpu.SemaphoreType.DMA((4, 16)),
        ],
        compiler_params=pltpu.CompilerParams(
            collective_id=0, has_side_effects=True, vmem_limit_bytes=63 << 20
        ),
    )(probes, kappa2, cotangents)


def solution(mesh):
    return jax.shard_map(
        body,
        mesh=mesh,
        in_specs=(P(None, "gx", "gy", "gz"), P("gx", "gy", "gz"), P()),
        out_specs=P("gx", "gy", "gz"),
        check_vma=False,
    )
```
